256 devices in a mesh: narrow: 8 (over y, z_lo), wide: 8 (over z_hi, core), nys: 4 (over x).
Axes of the slice: x: 4, y: 4, z: 8 (z_hi: 4, z_lo: 2; z = z_hi * 2 + z_lo), core: 2. Of those that a mesh axis runs over, the one named last changes fastest.
Arguments:
- centers: bfloat16 [262144, 1024], P(('narrow', 'wide', 'nys')), may hold values from -6 to 6
- weights: float32 [262144, 1000], P(('narrow', 'wide', 'nys')), may hold values from -6 to 6
- batch_points: bfloat16 [512, 1024], P(('narrow', 'wide', 'nys')), may hold values from -6 to 6
- labels: float32 [512, 1000], P(('narrow', 'wide', 'nys')), may hold values from -6 to 6
- nystrom_points: bfloat16 [2048, 1024], P(('narrow', 'nys')), may hold values from -6 to 6
- eigvecs: float32 [2048, 160], P(('narrow', 'nys')), may hold values from -0.125 to 0.125
- corrections: float32 [160], replicated, may hold values from 0.05 to 0.5
Outputs:
- new_weights: float32 [262144, 1000], P(('narrow', 'wide', 'nys'))
The draws below stay inside these ranges and needn't reach their ends.
All inputs are finite; a program needn't handle non-finite values.
Results may differ from the reference program's by a relative error of at most 0.0003.
The reference program's roundings to bfloat16 on the way (of `kernel`, `residual` and `corrected`) count: a program that leaves them out, or rounds other values in their place, can miss the bound.
Values may be sent and summed in bfloat16 or wider, within the bound.
A program may use at most 64 MiB of HBM per device.

```python
import math
import jax
import jax.numpy as jnp
from jax import lax

D = 1024
OUT = 1000
Q = 160
NYS = 2048
BATCH = 512
CEN_DEV = 1024
CENTERS = 262144


twin_count = 8


def spread_rows(key, rows):
    return jax.random.normal(jax.random.fold_in(key, 1), (rows, D), jnp.float32)


def drawn(key):
    base = jax.random.normal(jax.random.fold_in(key, 11), (2 * twin_count, D), jnp.float32)
    return jnp.clip(2.0 * base, -6.0, 6.0)


def twin_rows(key, plants):
    sigma = (math.sqrt(2.0 * D) - 4.0) / math.sqrt(D)
    noise = jax.random.normal(key, plants.shape, jnp.float32)
    return plants + sigma * noise


def draw_centers(key, part):
    values = spread_rows(jax.random.fold_in(key, 21), CENTERS)
    order = jax.random.permutation(jax.random.fold_in(key, 22), CENTERS)[:2 * twin_count]
    values = values.at[order].set(drawn(key))
    return jnp.clip(values, -6.0, 6.0).astype(jnp.bfloat16)


def draw_batch_points(key, part):
    values = spread_rows(jax.random.fold_in(key, 31), BATCH)
    order = jax.random.permutation(jax.random.fold_in(key, 32), BATCH)[:twin_count]
    twins = twin_rows(jax.random.fold_in(key, 33), drawn(key)[:twin_count])
    values = values.at[order].set(twins)
    return jnp.clip(values, -6.0, 6.0).astype(jnp.bfloat16)


def draw_nystrom_points(key, part):
    values = spread_rows(jax.random.fold_in(key, 41), NYS)
    order = jax.random.permutation(jax.random.fold_in(key, 42), NYS)[:twin_count]
    twins = twin_rows(jax.random.fold_in(key, 43), drawn(key)[twin_count:])
    values = values.at[order].set(twins)
    return jnp.clip(values, -6.0, 6.0).astype(jnp.bfloat16)


def block_levels(own_key, shape, cuts, smallest, largest):
    factor_of = 1.0
    for dim, blocks in cuts:
        draws = jax.random.uniform(jax.random.fold_in(jax.random.fold_in(own_key, 6), dim), (blocks,), jnp.float32, smallest / len(cuts), largest / len(cuts))
        factor_of = factor_of * jnp.repeat(jnp.exp(draws), shape[dim] // blocks).reshape((-1,) + (1,) * (len(shape) - 1 - dim))
    return factor_of


def bell_draw(rng, extent, width, bound, pieces=(), dtype=jnp.bfloat16):
    array = width * jax.random.normal(rng, extent, jnp.float32)
    if pieces:
        array = array * block_levels(rng, extent, pieces, -0.22, 0.18)
    return jnp.clip(array, -bound, bound).astype(dtype)


def setup_inputs(seed: int = 0) -> dict:
    key_of = jax.random.split(jax.random.key(seed), 8)
    return {
        "centers": draw_centers(jax.random.fold_in(key_of[7], 71), 0),
        "weights": bell_draw(key_of[1], (CENTERS, OUT), 1.0, 6.0, ((0, 256),), jnp.float32),
        "batch_points": draw_batch_points(jax.random.fold_in(key_of[7], 71), 0),
        "labels": bell_draw(key_of[3], (BATCH, OUT), 1.0, 6.0, ((0, 256),), jnp.float32),
        "nystrom_points": draw_nystrom_points(jax.random.fold_in(key_of[7], 71), 0),
        "eigvecs": bell_draw(key_of[5], (NYS, Q), NYS ** -0.5, 0.125, ((0, 32),), jnp.float32),
        "corrections": jnp.clip(jnp.exp(jax.random.uniform(key_of[6], (Q,), jnp.float32, math.log(0.05), math.log(0.5))), 0.05, 0.5),
    }


RATE = 16.0
SPREAD = 4.0

def kernel(left, right):
    cross = lax.dot_general(left, right, (((1,), (1,)), ((), ())), preferred_element_type=jnp.float32)
    left_sq = lax.optimization_barrier(jnp.sum(jnp.square(left.astype(jnp.float32)), axis=1))
    right_sq = lax.optimization_barrier(jnp.sum(jnp.square(right.astype(jnp.float32)), axis=1))
    dist = jnp.sqrt(jnp.maximum(left_sq[:, None] + right_sq[None, :] - 2.0 * cross, 0.0))
    radius = math.sqrt(2.0 * left.shape[1])
    return jnp.exp((radius - dist) / SPREAD).astype(jnp.bfloat16)

def reference(centers, weights, batch_points, labels, nystrom_points, eigvecs, corrections):
    blocks_c = centers.reshape(-1, CEN_DEV, D)
    blocks_w = weights.reshape(-1, CEN_DEV, OUT)

    def accumulate(total, pair):
        block_c, block_w = pair
        tile = kernel(block_c, batch_points)
        term = lax.dot_general(tile, block_w.astype(jnp.bfloat16), (((0,), (0,)), ((), ())), preferred_element_type=jnp.float32)
        return (total + term, None)
    total, _ = lax.scan(accumulate, jnp.zeros((BATCH, OUT), jnp.float32), (blocks_c, blocks_w))
    predicted = total * CENTERS ** (-0.5)
    residual = (predicted - labels).astype(jnp.bfloat16)
    pulled = jnp.dot(kernel(nystrom_points, batch_points), residual, preferred_element_type=jnp.float32)
    projected = lax.dot_general(eigvecs, pulled, (((0,), (0,)), ((), ())), precision=lax.Precision.HIGHEST)
    corrected = jnp.dot(eigvecs, corrections[:, None] * projected, precision=lax.Precision.HIGHEST).astype(jnp.bfloat16)

    def update(pair):
        block_c, block_w = pair
        gradient = jnp.dot(kernel(block_c, batch_points), residual, preferred_element_type=jnp.float32)
        nystrom_term = jnp.dot(kernel(block_c, nystrom_points), corrected, preferred_element_type=jnp.float32)
        return block_w - RATE / BATCH * (gradient - nystrom_term)
    return lax.map(update, (blocks_c, blocks_w)).reshape(CENTERS, OUT)
```

```python
import functools
import math

import jax
import jax.numpy as jnp
from jax import lax
from jax.experimental import pallas as pl
from jax.experimental.pallas import tpu as pltpu
from jax.sharding import PartitionSpec as P

RATE = 16.0
SPREAD = 4.0
MESH = pl.DeviceIdType.MESH


def place():
    n, w, x = (lax.axis_index(a) for a in ("narrow", "wide", "nys"))
    y, zl = n // 2, n % 2
    zh, c = w // 2, w % 2
    return x, y, zh * 2 + zl, c


def device(x, y, z, c):
    return (y * 2 + z % 2, (z // 2) * 2 + c, x)


class Links:
    def __init__(self):
        self.x, self.y, self.z, self.c = place()
        self.p = self.x * (1 - self.c) + self.y * self.c
        self.q = self.y * (1 - self.c) + self.x * self.c

    def core(self):
        return device(self.x, self.y, self.z, 1 - self.c)

    def along_p(self, k):
        c = self.c
        return device((self.x + k * (1 - c)) % 4, (self.y + k * c) % 4, self.z, c)

    def along_q(self, k):
        c = self.c
        return device((self.x + k * c) % 4, (self.y + k * (1 - c)) % 4, self.z, c)

    def along_z(self, k):
        return device(self.x, self.y, (self.z + k) % 8, self.c)

    def z_pair(self):
        return device(self.x, self.y, self.z + 1 - 2 * (self.z % 2), self.c)

    def greet(self):
        barrier = pltpu.get_barrier_semaphore()
        peers = [self.core()]
        peers += [self.along_p(k) for k in range(1, 4)]
        peers += [self.along_q(k) for k in range(1, 4)]
        peers += [self.along_z(k) for k in range(1, 8)]
        for peer in peers:
            pl.semaphore_signal(barrier, inc=1, device_id=peer, device_id_type=MESH)
        pl.semaphore_wait(barrier, len(peers))


class Copies:
    def __init__(self, send, recv):
        self.send, self.recv, self.next = send, recv, 0

    def start(self, pairs):
        out = []
        for src, dst, peer in pairs:
            copy = pltpu.make_async_remote_copy(
                src_ref=src,
                dst_ref=dst,
                send_sem=self.send.at[self.next],
                recv_sem=self.recv.at[self.next],
                device_id=peer,
                device_id_type=MESH,
            )
            self.next += 1
            copy.start()
            out.append(copy)
        return out


def arrived(copies):
    for copy in copies:
        copy.wait_recv()


def sent(copies):
    for copy in copies:
        copy.wait_send()


def rows(ref, start, size, unit):
    return ref.at[pl.ds(pl.multiple_of(start, unit), size), :]


def gather_tiles(links, copies, ref):
    c, p, q, z = links.c, links.p, links.q, links.z
    tile = ref.at[
        pl.ds(pl.multiple_of(c * 256 + p * 64 + q * 16, 16), 16),
        pl.ds(pl.multiple_of(z * 128, 128), 128),
    ]
    out = copies.start([(tile, tile, links.along_z(k)) for k in range(1, 8)])
    yield out
    arrived(out)
    block = rows(ref, c * 256 + p * 64 + q * 16, 16, 16)
    out = copies.start([(block, block, links.along_q(k)) for k in range(1, 4)])
    yield out
    arrived(out)
    block = rows(ref, c * 256 + p * 64, 64, 64)
    out = copies.start([(block, block, links.along_p(k)) for k in range(1, 4)])
    yield out
    arrived(out)
    block = rows(ref, c * 256, 256, 256)
    out = copies.start([(block, block, links.core())])
    yield out
    arrived(out)
    yield []


def gather_shards(links, copies, refs):
    c, p, q, zl = links.c, links.p, links.q, links.z % 2
    own = [rows(r, c * 1024 + p * 256 + q * 64 + zl * 32, 32, 32) for r in refs]
    out = copies.start([(o, o, links.z_pair()) for o in own])
    yield out
    arrived(out)
    own = [rows(r, c * 1024 + p * 256 + q * 64, 64, 64) for r in refs]
    out = copies.start([(o, o, links.along_q(k)) for k in range(1, 4) for o in own])
    yield out
    arrived(out)
    own = [rows(r, c * 1024 + p * 256, 256, 256) for r in refs]
    out = copies.start([(o, o, links.along_p(k)) for k in range(1, 4) for o in own])
    yield out
    arrived(out)
    own = [rows(r, c * 1024, 1024, 1024) for r in refs]
    out = copies.start([(o, o, links.core()) for o in own])
    yield out
    arrived(out)
    yield []


def gather_kernel(batch, nystrom, eig, batch_all, nystrom_all, eig_all, send, recv):
    links = Links()
    c, p, q, z = links.c, links.p, links.q, links.z
    row, col = c * 256 + p * 64 + q * 16, z * 128
    batch_all[pl.ds(pl.multiple_of(row, 16), 16), pl.ds(pl.multiple_of(col, 128), 128)] = batch[...]
    row = pl.multiple_of(c * 1024 + p * 256 + q * 64 + (z % 2) * 32, 32)
    half = pl.ds(pl.multiple_of(c * 32, 32), 32)
    nystrom_all[pl.ds(row, 32), :] = nystrom[half, :]
    eig_all[pl.ds(row, 32), :] = eig[half, :]
    links.greet()
    copies = Copies(send, recv)
    first = gather_tiles(links, copies, batch_all)
    second = gather_shards(links, copies, (nystrom_all, eig_all))
    started = []
    for _ in range(5):
        started += next(first)
        started += next(second)
    sent(started)


def gather(batch, nystrom, eig):
    vmem = pl.BlockSpec(memory_space=pltpu.VMEM)
    return pl.pallas_call(
        gather_kernel,
        out_shape=(
            jax.ShapeDtypeStruct((512, 1024), jnp.bfloat16),
            jax.ShapeDtypeStruct((2048, 1024), jnp.bfloat16),
            jax.ShapeDtypeStruct((2048, 256), jnp.float32),
        ),
        in_specs=[vmem] * 3,
        out_specs=(vmem,) * 3,
        scratch_shapes=[pltpu.SemaphoreType.DMA((30,)), pltpu.SemaphoreType.DMA((30,))],
        compiler_params=pltpu.CompilerParams(
            collective_id=0, has_side_effects=True, vmem_limit_bytes=40 << 20
        ),
        name="gather",
    )(batch, nystrom, eig)


def add_up(out, terms):
    count = out.shape[0]
    step = min(count, 16)

    def body(i, carry):
        at = pl.ds(pl.multiple_of(i * step, step), step)
        total = terms[0][at, :]
        for term in terms[1:]:
            total = total + term[at, :]
        out[at, :] = total.astype(out.dtype)
        return carry

    lax.fori_loop(0, count // step, body, 0)


def reduce_kernel(part, labels, resid, sum0, sum1, sum2, from_core, from_p, from_q, from_z, send, recv):
    links = Links()
    c, p, q, z = links.c, links.p, links.q, links.z
    group = c * 16 + p * 4 + q
    links.greet()
    copies = Copies(send, recv)
    started = out = copies.start([(rows(part, (1 - c) * 256, 256, 256), from_core, links.core())])
    arrived(out)
    add_up(sum0, [rows(part, c * 256, 256, 256), from_core])
    out = copies.start(
        [
            (rows(sum0, ((p + k) % 4) * 64, 64, 64), from_p.at[k - 1], links.along_p(k))
            for k in range(1, 4)
        ]
    )
    started += out
    arrived(out)
    add_up(sum1, [rows(sum0, p * 64, 64, 64)] + [from_p.at[k] for k in range(3)])
    out = copies.start(
        [
            (rows(sum1, ((q + k) % 4) * 16, 16, 16), from_q.at[k - 1], links.along_q(k))
            for k in range(1, 4)
        ]
    )
    started += out
    arrived(out)
    line = lax.broadcasted_iota(jnp.int32, (16, 1024), 0) - z * 2
    placed = jnp.where(line == 0, labels[0:1, :], jnp.where(line == 1, labels[1:2, :], 0.0))
    total = sum1[pl.ds(pl.multiple_of(q * 16, 16), 16), :] - placed
    for k in range(3):
        total = total + from_q[k]
    sum2[...] = total
    out = copies.start(
        [
            (
                sum2.at[:, pl.ds(pl.multiple_of(((z + k) % 8) * 128, 128), 128)],
                from_z.at[k - 1],
                links.along_z(k),
            )
            for k in range(1, 8)
        ]
    )
    started += out
    arrived(out)
    total = sum2[:, pl.ds(pl.multiple_of(z * 128, 128), 128)]
    for k in range(7):
        total = total + from_z[k]
    resid[
        pl.ds(pl.multiple_of(group * 16, 16), 16), pl.ds(pl.multiple_of(z * 128, 128), 128)
    ] = total.astype(resid.dtype)
    for out in gather_tiles(links, copies, resid):
        started += out
    sent(started)


def reduce(part, labels):
    vmem = pl.BlockSpec(memory_space=pltpu.VMEM)
    return pl.pallas_call(
        reduce_kernel,
        out_shape=jax.ShapeDtypeStruct((512, 1024), jnp.bfloat16),
        in_specs=[vmem] * 2,
        out_specs=vmem,
        scratch_shapes=[
            pltpu.VMEM((256, 1024), jnp.float32),
            pltpu.VMEM((64, 1024), jnp.float32),
            pltpu.VMEM((16, 1024), jnp.float32),
            pltpu.VMEM((256, 1024), jnp.float32),
            pltpu.VMEM((3, 64, 1024), jnp.float32),
            pltpu.VMEM((3, 16, 1024), jnp.float32),
            pltpu.VMEM((7, 16, 128), jnp.float32),
            pltpu.SemaphoreType.DMA((28,)),
            pltpu.SemaphoreType.DMA((28,)),
        ],
        compiler_params=pltpu.CompilerParams(
            collective_id=1, has_side_effects=True, vmem_limit_bytes=40 << 20
        ),
        name="reduce",
    )(part, labels)


def kernel_of(left, left_sq, right, right_sq):
    cross = lax.dot_general(
        left, right, (((1,), (1,)), ((), ())), preferred_element_type=jnp.float32
    )
    dist = jnp.sqrt(jnp.maximum(left_sq[:, None] + right_sq[None, :] - 2.0 * cross, 0.0))
    radius = math.sqrt(2.0 * left.shape[1])
    return jnp.exp((radius - dist) / SPREAD).astype(jnp.bfloat16)


def squares(points):
    return jnp.sum(jnp.square(points.astype(jnp.float32)), axis=1)


def per_device(centers, weights, batch_points, labels, nystrom_points, eigvecs, corrections):
    outs = weights.shape[1]
    scale = (centers.shape[0] * 256) ** (-0.5)
    tiles, points, eig = gather(
        batch_points.reshape(16, 128),
        nystrom_points,
        jnp.pad(eigvecs, ((0, 0), (0, 256 - eigvecs.shape[1]))),
    )
    eig = eig[:, : eigvecs.shape[1]]
    batch = tiles.reshape(32, 2, 8, 8, 128).transpose(0, 3, 1, 2, 4).reshape(512, 1024)
    center_sq, batch_sq, points_sq = squares(centers), squares(batch), squares(points)
    k_batch = kernel_of(centers, center_sq, batch, batch_sq)
    part = (
        lax.dot_general(
            k_batch,
            weights.astype(jnp.bfloat16),
            (((0,), (0,)), ((), ())),
            preferred_element_type=jnp.float32,
        )
        * scale
    )
    wide = ((0, 0), (0, 1024 - outs))
    resid = reduce(jnp.pad(part, wide), jnp.pad(labels, wide))[:, :outs]
    k_nystrom = kernel_of(points, points_sq, batch, batch_sq)
    pulled = jnp.dot(k_nystrom, resid, preferred_element_type=jnp.float32)
    projected = lax.dot_general(
        eig, pulled, (((0,), (0,)), ((), ())), precision=lax.Precision.HIGHEST
    )
    gradient = jnp.dot(k_batch, resid, preferred_element_type=jnp.float32)
    corrected = jnp.dot(
        eig, corrections[:, None] * projected, precision=lax.Precision.HIGHEST
    ).astype(jnp.bfloat16)
    tile = kernel_of(centers, center_sq, points, points_sq)
    nystrom_term = jnp.dot(tile, corrected, preferred_element_type=jnp.float32)
    return weights - RATE / 512 * (gradient - nystrom_term)


def solution(mesh):
    every = P(("narrow", "wide", "nys"), None)
    some = P(("narrow", "nys"), None)
    return jax.shard_map(
        per_device,
        mesh=mesh,
        in_specs=(every, every, every, every, some, some, P()),
        out_specs=every,
        check_vma=False,
    )
```

```python
import math

import jax
import jax.numpy as jnp
from jax import lax
from jax.experimental import pallas as pl
from jax.experimental.pallas import tpu as pltpu
from jax.sharding import PartitionSpec as P

RATE = 16.0
SPREAD = 4.0
MESH = pl.DeviceIdType.MESH
F32, BF16 = jnp.float32, jnp.bfloat16

FEATURES = 1024
CEN = 1024
OUT = 1000
NYS = 2048
BATCH = 512
Q = 160
UNIT = (math.log2(math.e) / SPREAD) ** 2
TOP = math.sqrt(2.0 * FEATURES) * math.log2(math.e) / SPREAD


def device(x, y, z, c):
    return (y * 2 + z % 2, (z // 2) * 2 + c, x)


class Links:
    def __init__(self, send, recv):
        n, w, self.x = (lax.axis_index(a) for a in ("narrow", "wide", "nys"))
        self.y, self.c = n // 2, w % 2
        self.z = (w // 2) * 2 + n % 2
        self.p = self.x * (1 - self.c) + self.y * self.c
        self.q = self.y * (1 - self.c) + self.x * self.c
        self.send, self.recv, self.next, self.all = send, recv, 0, []

    def core(self):
        return device(self.x, self.y, self.z, 1 - self.c)

    def along_p(self, k):
        c = self.c
        return device((self.x + k * (1 - c)) % 4, (self.y + k * c) % 4, self.z, c)

    def along_q(self, k):
        c = self.c
        return device((self.x + k * c) % 4, (self.y + k * (1 - c)) % 4, self.z, c)

    def along_z(self, k):
        return device(self.x, self.y, (self.z + k) % 8, self.c)

    def z_pair(self):
        return device(self.x, self.y, self.z + 1 - 2 * (self.z % 2), self.c)

    def peers(self):
        out = [self.core()]
        out += [self.along_p(k) for k in range(1, 4)]
        out += [self.along_q(k) for k in range(1, 4)]
        out += [self.along_z(k) for k in range(1, 8)]
        return out

    def start(self, pairs):
        out = []
        for src, dst, peer in pairs:
            copy = pltpu.make_async_remote_copy(
                src_ref=src,
                dst_ref=dst,
                send_sem=self.send.at[self.next],
                recv_sem=self.recv.at[self.next],
                device_id=peer,
                device_id_type=MESH,
            )
            self.next += 1
            copy.start()
            out.append(copy)
        self.all += out
        return out


def arrived(copies):
    for copy in copies:
        copy.wait_recv()


def at(start, size, unit=None):
    if isinstance(start, int):
        return slice(start, start + size)
    return pl.ds(pl.multiple_of(start, unit or size), size)


def square_sums(points):
    wide = points.astype(F32)
    return jnp.sum(wide * wide, axis=1, keepdims=True) * UNIT


def as_row(column):
    return jnp.transpose(jnp.broadcast_to(column, (column.shape[0], 128)))[0:1, :]


def kernel_values(left, left_sq, right, right_sq):
    cross = lax.dot_general(left, right, (((1,), (1,)), ((), ())), preferred_element_type=F32)
    dist_sq = jnp.maximum((left_sq + right_sq) - (2.0 * UNIT) * cross, 1e-30)
    return jnp.exp2(TOP - dist_sq * lax.rsqrt(dist_sq)).astype(BF16)


def three(value):
    high = value.astype(BF16)
    rest = value - high.astype(F32)
    middle = rest.astype(BF16)
    low = (rest - middle.astype(F32)).astype(BF16)
    return high, middle, low


def step_kernel(
    centers,
    weights,
    batch,
    labels,
    nystrom,
    eigvecs,
    corrections,
    out,
    left,
    left_sq,
    right,
    right_sq,
    center_sq,
    small_batch,
    small_labels,
    small_eig,
    small_corr,
    tiles,
    wide_tiles,
    wide_batch,
    old,
    rounded,
    eig,
    stack,
    k_batch,
    part,
    sum1,
    sum2,
    from_p,
    from_q,
    from_z,
    table,
    mixed,
    mixed_t,
    coefs,
    tail_in,
    send,
    recv,
    local,
):
    links = Links(send, recv)
    c, p, q, z = links.c, links.p, links.q, links.z
    group = p * 4 + q

    own_n = c * 1024 + p * 256 + q * 64 + (z % 2) * 32
    loads = [
        (batch, small_batch),
        (labels, small_labels),
        (eigvecs, small_eig),
        (nystrom.at[at(c * 32, 32), :], right.at[at(own_n, 32), :]),
        (centers, left.at[0:1024, :]),
        (weights, old),
        (corrections, small_corr),
    ]
    loads = [pltpu.make_async_copy(s, d, local.at[i]) for i, (s, d) in enumerate(loads)]
    for load in loads:
        load.start()
    barrier = pltpu.get_barrier_semaphore()
    peers = links.peers()
    for peer in peers:
        pl.semaphore_signal(barrier, inc=1, device_id=peer, device_id_type=MESH)

    loads[0].wait()
    pair = small_batch[...].astype(F32)
    for r in range(2):
        for j in range(8):
            wide_tiles[0, 8 * r + j : 8 * r + j + 1, :] = pair[r : r + 1, 128 * j : 128 * j + 128]
    tiles[at(group * 16, 16), at(z * 128, 128)] = wide_tiles[0, 0:16, :].astype(BF16)
    loads[1].wait()
    loads[2].wait()
    eig[at(own_n, 32), :] = jnp.zeros((32, 256), F32)
    eig[at(own_n, 32), 0:Q] = small_eig[at(c * 32, 32), :]
    loads[3].wait()
    pl.semaphore_wait(barrier, len(peers))

    def gather_z(ref, first):
        tile = ref.at[at(first + group * 16, 16), at(z * 128, 128)]
        return links.start([(tile, tile, links.along_z(k)) for k in range(1, 8)])

    def gather_q(ref, first):
        block = ref.at[at(first + group * 16, 16), :]
        return links.start([(block, block, links.along_q(k)) for k in range(1, 4)])

    def gather_p(ref, first):
        block = ref.at[at(first + p * 64, 64), :]
        return links.start([(block, block, links.along_p(k)) for k in range(1, 4)])

    batch_z = gather_z(tiles, 0)
    own = [r.at[at(own_n, 32), :] for r in (right, eig)]
    nys_z = links.start([(o, o, links.z_pair()) for o in own])
    loads[4].wait()
    swap = links.start([(left.at[0:1024, :], left.at[1280:2304, :], links.core())])

    arrived(batch_z)
    batch_q = gather_q(tiles, 0)
    arrived(nys_z)
    own = [r.at[at(c * 1024 + p * 256 + q * 64, 64), :] for r in (right, eig)]
    nys_q = links.start([(o, o, links.along_q(k)) for k in range(1, 4) for o in own])

    loads[5].wait()
    rounded[0:1024, 896:1024] = jnp.zeros((1024, 128), BF16)

    def round_rows(i, carry):
        rows = at(i * 128, 128)
        rounded[rows, 0:OUT] = old[rows, :].astype(BF16)
        return carry

    lax.fori_loop(0, 8, round_rows, 0)
    swap += links.start([(rounded.at[0:1024, :], rounded.at[1024:2048, :], links.core())])

    arrived(batch_q)
    batch_p = gather_p(tiles, 0)

    def own_squares(i, carry):
        rows = at(i * 256, 256)
        value = square_sums(left[rows, :])
        left_sq[rows, :] = value
        center_sq[:, rows] = as_row(value)
        return carry

    lax.fori_loop(0, 4, own_squares, 0)
    arrived(nys_q)
    blocks = [c * 1024 + ((p + k) % 4) * 256 for k in range(4)]
    block = right.at[at(blocks[0], 256), :]
    nys_own = links.start([(block, block, links.core())])
    arrived(swap)

    def other_squares(i, carry):
        rows = pl.ds(pl.multiple_of(1280 + i * 256, 256), 256)
        center_sq[:, at(1024 + i * 256, 256)] = as_row(square_sums(left[rows, :]))
        return carry

    lax.fori_loop(0, 4, other_squares, 0)
    arrived(batch_p)
    own = [r.at[at(blocks[0], 256), :] for r in (right, eig)]
    nys_p = links.start([(o, o, links.along_p(k)) for k in (1, 3) for o in own[:1]])
    eig_p = links.start([(own[1], own[1], links.along_p(k)) for k in (1, 2, 3)])

    for zz in range(8):
        wide_tiles[zz] = tiles[:, 128 * zz : 128 * zz + 128].astype(F32)
    for zz in range(8):
        for j in range(8):
            wide_batch[j, pl.ds(zz, 32, stride=8), :] = wide_tiles[zz, pl.ds(j, 32, stride=8), :]
    squares = jnp.zeros((256, 128), F32)
    for j in range(8):
        wide = wide_batch[j]
        left[1024:1280, 128 * j : 128 * j + 128] = wide.astype(BF16)
        squares = squares + wide * wide
    left_sq[1024:1280, :] = jnp.sum(squares, axis=1, keepdims=True) * UNIT
    right[at(2048 + c * 256, 256), :] = left[1024:1280, :]
    block = right.at[at(2048 + c * 256, 256), :]
    batch_own = links.start([(block, block, links.core())])
    points, points_sq = left[1024:1280, :], left_sq[1024:1280, :]
    for i in range(8):
        first = i * 256 if i < 4 else 256 + i * 256
        k_batch[:, 256 * i : 256 * i + 256] = kernel_values(
            points, points_sq, left[first : first + 256, :], center_sq[:, 256 * i : 256 * i + 256]
        )
    scale = (CEN * 256) ** (-0.5)
    for i in range(4):
        cols = slice(256 * i, 256 * i + 256)
        part[:, cols] = scale * jnp.dot(k_batch[...], rounded[:, cols], preferred_element_type=F32)
    sum_p = links.start(
        [
            (part.at[at(((p + k) % 4) * 64, 64), :], from_p.at[k - 1], links.along_p(k))
            for k in range(1, 4)
        ]
    )

    def fill(first, height):
        cols = at(first, 256)
        if not isinstance(first, int):
            cols = pl.ds(pl.multiple_of(first, 256), 256)
        right_sq[:, cols] = as_row(square_sums(right[cols, :]))

        def body(i, carry):
            rows = at(i * (height // 2), height // 2)
            table[rows, cols] = kernel_values(
                left[rows, :], left_sq[rows, :], right[cols, :], right_sq[:, cols]
            )
            return carry

        lax.fori_loop(0, 2, body, 0)

    theirs = [(1 - c) * 1024 + ((q + k) % 4) * 256 for k in range(4)]
    fill(blocks[0], 1280)
    arrived(nys_own)
    fill(theirs[0], 1280)
    arrived(nys_p)
    nys_core = links.start(
        [
            (right.at[at(blocks[k], 256), :], right.at[at(blocks[k], 256), :], links.core())
            for k in (1, 3)
        ]
    )
    fill(blocks[1], 1280)
    fill(blocks[3], 1280)
    arrived(batch_own)

    arrived(sum_p)
    nys_far = links.start([(own[0], own[0], links.along_p(2))])
    arrived(eig_p)
    half = eig.at[at(c * 1024, 1024), :]
    eig_core = links.start([(half, half, links.core())])

    def add_p(i, carry):
        rows = at(i * 16, 16)
        sum1[rows, :] = (
            part[at(p * 64 + i * 16, 16), :]
            + from_p[0, rows, :]
            + from_p[1, rows, :]
            + from_p[2, rows, :]
        )
        return carry

    lax.fori_loop(0, 4, add_p, 0)
    line = lax.broadcasted_iota(jnp.int32, (16, OUT), 0)
    placed = jnp.where(
        line == z, small_labels[0:1, :], jnp.where(line == z + 8, small_labels[1:2, :], 0.0)
    )
    sum1[at(q * 16, 16), 0:OUT] = sum1[at(q * 16, 16), 0:OUT] - placed
    sum_q = links.start(
        [
            (sum1.at[at(((q + k) % 4) * 16, 16), :], from_q.at[k - 1], links.along_q(k))
            for k in range(1, 4)
        ]
    )
    arrived(nys_core)
    fill(theirs[1], 1280)
    fill(theirs[3], 1280)
    arrived(sum_q)
    sum2[...] = sum1[at(q * 16, 16), :] + from_q[0] + from_q[1] + from_q[2]
    sum_z = links.start(
        [
            (sum2.at[:, at(((z + k) % 8) * 128, 128)], from_z.at[k - 1], links.along_z(k))
            for k in range(1, 8)
        ]
    )
    arrived(nys_far)
    block = right.at[at(blocks[2], 256), :]
    nys_last = links.start([(block, block, links.core())])
    fill(2048, 1024)
    fill(2304, 1024)
    fill(blocks[2], 1280)
    arrived(sum_z)
    total = sum2[:, at(z * 128, 128)]
    for k in range(7):
        total = total + from_z[k]
    coefs[at(2048 + c * 256 + group * 16, 16), at(z * 128, 128)] = total.astype(BF16)
    first = 2048 + c * 256
    resid_z = gather_z(coefs, first)

    arrived(nys_last)
    fill(theirs[2], 1280)
    arrived(eig_core)

    def split(i, carry):
        rows = at(i * 256, 256)
        a = three(eig[rows, 0:128])
        high, middle, low = (v.astype(F32) for v in three(eig[rows, 128:256]))
        for j, v in enumerate((0, 0, 1, 0, 1, 2)):
            stack[rows, 128 * j : 128 * j + 128] = a[v]
        stack[rows, 768:896] = (
            high
            + pltpu.roll(high, 32, 1)
            + pltpu.roll(middle, 64, 1)
            + pltpu.roll(high, 96, 1)
        ).astype(BF16)
        stack[rows, 896:1024] = (middle + pltpu.roll(low, 32, 1)).astype(BF16)
        return carry

    lax.fori_loop(0, 8, split, 0)
    arrived(resid_z)
    resid_q = gather_q(coefs, first)

    loads[6].wait()
    mixed_rows = at(c * 256, 256)
    product = jnp.dot(table[1024:1280, 0:NYS], stack[...], preferred_element_type=F32)
    mixed[mixed_rows, 0:128] = (
        product[:, 0:128] + product[:, 256:384] + product[:, 640:768]
    ) * small_corr[:, 0:128]
    last = product[:, 768:896]
    last = last + pltpu.roll(last, 64, 1) + pltpu.roll(product[:, 896:1024], 96, 1)
    mixed[mixed_rows, 128:Q] = last[:, 0 : Q - 128] * small_corr[:, 128:Q]
    half = mixed.at[mixed_rows, :]
    mixed_core = links.start([(half, half, links.core())])
    arrived(resid_q)
    resid_p = gather_p(coefs, first)
    block = coefs.at[at(first + p * 64, 64), :]
    resid_core = links.start([(block, block, links.core())])
    arrived(mixed_core)
    turned = jnp.transpose(mixed[...])[0:Q, :]
    for i, piece in enumerate(three(turned)):
        mixed_t[Q * i : Q * i + Q, :] = piece
    for k, copy in zip((1, 2, 3), resid_p):
        arrived([copy])
        block = coefs.at[at(first + ((p + 4 - k) % 4) * 64, 64), :]
        resid_core += links.start([(block, block, links.core())])
    arrived(resid_core)

    for i in range(4):
        cols = slice(256 * i, 256 * i + 256)
        resid = coefs[2048:2560, cols]
        pieces = jnp.dot(mixed_t[...], resid, preferred_element_type=F32)
        pieces = three(pieces[0:Q] + pieces[Q : 2 * Q] + pieces[2 * Q : 3 * Q])
        for j, v in enumerate((0, 1, 0, 2, 1, 0)):
            tail_in[128 * j : 128 * j + 128, :] = pieces[v][0:128]
            tail_in[768 + 32 * j : 800 + 32 * j, :] = pieces[v][128:Q]
        tail_in[960:1024, :] = jnp.zeros((64, 256), BF16)

        def correct(k, carry):
            rows = at(k * 512, 512)
            coefs[rows, cols] = -jnp.dot(
                stack[rows, :], tail_in[...], preferred_element_type=F32
            ).astype(BF16)
            return carry

        lax.fori_loop(0, 4, correct, 0)
        kept = slice(256 * i, min(256 * i + 256, OUT))

        def finish(k, carry):
            rows = at(k * 512, 512)
            change = jnp.dot(table[rows, :], coefs[:, cols], preferred_element_type=F32)
            out[rows, kept] = old[rows, kept] - (RATE / BATCH) * change[:, 0 : kept.stop - kept.start]
            return carry

        lax.fori_loop(0, 2, finish, 0)
    for copy in links.all:
        copy.wait_send()


def per_device(centers, weights, batch_points, labels, nystrom_points, eigvecs, corrections):
    anywhere = pl.BlockSpec(memory_space=pl.ANY)
    vmem = pltpu.VMEM
    return pl.pallas_call(
        step_kernel,
        out_shape=jax.ShapeDtypeStruct((CEN, OUT), F32),
        in_specs=[anywhere] * 7,
        out_specs=pl.BlockSpec(memory_space=vmem),
        scratch_shapes=[
            vmem((2304, FEATURES), BF16),
            vmem((1280, 1), F32),
            vmem((2560, FEATURES), BF16),
            vmem((1, 2560), F32),
            vmem((1, 2048), F32),
            vmem((2, FEATURES), BF16),
            vmem((2, OUT), F32),
            vmem((64, Q), F32),
            vmem((1, Q), F32),
            vmem((256, FEATURES), BF16),
            vmem((8, 256, 128), F32),
            vmem((8, 256, 128), F32),
            vmem((CEN, OUT), F32),
            vmem((2048, 1024), BF16),
            vmem((NYS, 256), F32),
            vmem((NYS, 1024), BF16),
            vmem((256, 2048), BF16),
            vmem((256, 1024), F32),
            vmem((64, 1024), F32),
            vmem((16, 1024), F32),
            vmem((3, 64, 1024), F32),
            vmem((3, 16, 1024), F32),
            vmem((7, 16, 128), F32),
            vmem((1280, 2560), BF16),
            vmem((BATCH, 256), F32),
            vmem((3 * Q, BATCH), BF16),
            vmem((2560, 1024), BF16),
            vmem((1024, 256), BF16),
            pltpu.SemaphoreType.DMA((80,)),
            pltpu.SemaphoreType.DMA((80,)),
            pltpu.SemaphoreType.DMA((7,)),
        ],
        compiler_params=pltpu.CompilerParams(
            collective_id=0, has_side_effects=True, vmem_limit_bytes=60 << 20
        ),
        name="step",
    )(
        centers,
        weights,
        batch_points,
        labels,
        nystrom_points,
        eigvecs,
        corrections.reshape(1, Q),
    )


def solution(mesh):
    every = P(("narrow", "wide", "nys"), None)
    some = P(("narrow", "nys"), None)
    return jax.shard_map(
        per_device,
        mesh=mesh,
        in_specs=(every, every, every, every, some, some, P()),
        out_specs=every,
        check_vma=False,
    )
```

```python
import math

import jax
import jax.numpy as jnp
from jax import lax
from jax.experimental import pallas as pl
from jax.experimental.pallas import tpu as pltpu
from jax.sharding import PartitionSpec as P

RATE = 16.0
SPREAD = 4.0
MESH = pl.DeviceIdType.MESH
F32, BF16 = jnp.float32, jnp.bfloat16

FEATURES = 1024
CEN = 1024
OUT = 1000
NYS = 2048
BATCH = 512
Q = 160
UNIT = (math.log2(math.e) / SPREAD) ** 2
TOP = math.sqrt(2.0 * FEATURES) * math.log2(math.e) / SPREAD


def device(x, y, z, c):
    return (y * 2 + z % 2, (z // 2) * 2 + c, x)


class Links:
    def __init__(self, send, recv):
        n, w, self.x = (lax.axis_index(a) for a in ("narrow", "wide", "nys"))
        self.y, self.c = n // 2, w % 2
        self.z = (w // 2) * 2 + n % 2
        self.p = self.x * (1 - self.c) + self.y * self.c
        self.q = self.y * (1 - self.c) + self.x * self.c
        self.send, self.recv, self.next, self.all = send, recv, 0, []

    def core(self):
        return device(self.x, self.y, self.z, 1 - self.c)

    def along_p(self, k):
        c = self.c
        return device((self.x + k * (1 - c)) % 4, (self.y + k * c) % 4, self.z, c)

    def along_q(self, k):
        c = self.c
        return device((self.x + k * c) % 4, (self.y + k * (1 - c)) % 4, self.z, c)

    def along_z(self, k):
        return device(self.x, self.y, (self.z + k) % 8, self.c)

    def z_pair(self):
        return device(self.x, self.y, self.z + 1 - 2 * (self.z % 2), self.c)

    def peers(self):
        out = [self.core()]
        out += [self.along_p(k) for k in range(1, 4)]
        out += [self.along_q(k) for k in range(1, 4)]
        out += [self.along_z(k) for k in range(1, 8)]
        return out

    def start(self, pairs):
        out = []
        for src, dst, peer in pairs:
            copy = pltpu.make_async_remote_copy(
                src_ref=src,
                dst_ref=dst,
                send_sem=self.send.at[self.next],
                recv_sem=self.recv.at[self.next],
                device_id=peer,
                device_id_type=MESH,
            )
            self.next += 1
            copy.start()
            out.append(copy)
        self.all += out
        return out


def arrived(copies):
    for copy in copies:
        copy.wait_recv()


def at(start, size, unit=None):
    if isinstance(start, int):
        return slice(start, start + size)
    return pl.ds(pl.multiple_of(start, unit or size), size)


def square_sums(points):
    wide = points.astype(F32)
    return jnp.sum(wide * wide, axis=1, keepdims=True) * UNIT


def as_row(column):
    return jnp.transpose(jnp.broadcast_to(column, (column.shape[0], 128)))[0:1, :]


def kernel_values(left, left_sq, right, right_sq):
    cross = lax.dot_general(left, right, (((1,), (1,)), ((), ())), preferred_element_type=F32)
    dist_sq = jnp.maximum((left_sq + right_sq) - (2.0 * UNIT) * cross, 1e-30)
    return jnp.exp2(TOP - dist_sq * lax.rsqrt(dist_sq)).astype(BF16)


def three(value):
    high = value.astype(BF16)
    rest = value - high.astype(F32)
    middle = rest.astype(BF16)
    low = (rest - middle.astype(F32)).astype(BF16)
    return high, middle, low


def step_kernel(
    centers,
    weights,
    batch,
    labels,
    nystrom,
    eigvecs,
    corrections,
    out,
    left,
    left_sq,
    right,
    right_sq,
    center_sq,
    small_batch,
    small_labels,
    small_eig,
    small_corr,
    tiles,
    wide_tiles,
    wide_batch,
    old,
    rounded,
    eig,
    stack,
    k_batch,
    part,
    placed,
    sum1,
    sum2,
    from_p,
    from_q,
    from_z,
    table,
    mixed,
    coefs,
    scaled,
    send,
    recv,
    local,
):
    links = Links(send, recv)
    c, p, q, z = links.c, links.p, links.q, links.z
    group = p * 4 + q

    own_n = c * 1024 + p * 256 + q * 64 + (z % 2) * 32
    loads = [
        (batch, small_batch),
        (labels, small_labels),
        (eigvecs, small_eig),
        (nystrom.at[at(c * 32, 32), :], right.at[at(own_n, 32), :]),
        (centers, left.at[0:1024, :]),
        (weights, old),
        (corrections, small_corr),
    ]
    loads = [pltpu.make_async_copy(s, d, local.at[i]) for i, (s, d) in enumerate(loads)]
    for load in loads:
        load.start()
    barrier = pltpu.get_barrier_semaphore()
    peers = links.peers()
    for peer in peers:
        pl.semaphore_signal(barrier, inc=1, device_id=peer, device_id_type=MESH)

    loads[0].wait()
    pair = small_batch[...].astype(F32)
    for r in range(2):
        for j in range(8):
            wide_tiles[0, 8 * r + j : 8 * r + j + 1, :] = pair[r : r + 1, 128 * j : 128 * j + 128]
    tiles[at(group * 16, 16), at(z * 128, 128)] = wide_tiles[0, 0:16, :].astype(BF16)
    loads[2].wait()
    own_e = own_n // 32
    mine = small_eig[at(c * 32, 32), :]
    eig[own_e, 0:32, :] = mine[:, 0:128]
    for k in range(4):
        eig[own_e, 32:40, 32 * k : 32 * k + 32] = mine[8 * k : 8 * k + 8, 128:Q]
    loads[3].wait()
    pl.semaphore_wait(barrier, len(peers))

    def nys(first, count):
        return right.at[at(first, count, count), :]

    def vectors(first, count):
        return eig.at[pl.ds(first // 32, count // 32)]

    tile = tiles.at[at(group * 16, 16), at(z * 128, 128)]
    batch_q = links.start([(tile, tile, links.along_q(k)) for k in range(1, 4)])
    own = [nys(own_n, 32), vectors(own_n, 32)]
    nys_z = links.start([(o, o, links.z_pair()) for o in own])
    loads[4].wait()
    swap = links.start([(left.at[0:1024, :], left.at[1280:2304, :], links.core())])

    arrived(batch_q)
    tile = tiles.at[at(p * 64, 64), at(z * 128, 128)]
    batch_z = links.start([(tile, tile, links.along_z(k)) for k in range(1, 8)])
    arrived(nys_z)
    own_q = c * 1024 + p * 256 + q * 64
    own = [nys(own_q, 64), vectors(own_q, 64)]
    nys_q = links.start([(o, o, links.along_q(k)) for k in range(1, 4) for o in own])

    loads[5].wait()
    for i in range(7):
        rows = slice(128 * i, 128 * i + 128)
        rounded[rows, 0:1024] = old[rows, :].astype(BF16)
    last = jnp.concatenate([old[896:OUT, :], jnp.zeros((1024 - OUT, CEN), F32)], axis=0)
    rounded[896:1024, 0:1024] = last.astype(BF16)
    swap += links.start([(rounded.at[:, 0:1024], rounded.at[:, 1024:2048], links.core())])

    arrived(batch_z)
    block = tiles.at[at(p * 64, 64), :]
    batch_p = links.start([(block, block, links.along_p(k)) for k in range(1, 4)])

    def own_squares(i, carry):
        rows = at(i * 256, 256)
        value = square_sums(left[rows, :])
        left_sq[rows, :] = value
        center_sq[:, rows] = as_row(value)
        return carry

    lax.fori_loop(0, 4, own_squares, 0)
    loads[1].wait()
    wide_labels = [
        jnp.transpose(jnp.broadcast_to(small_labels[r : r + 1, :], (128, OUT))) for r in range(2)
    ]
    lane = lax.broadcasted_iota(jnp.int32, (OUT, 128), 1)
    for i in range(2):
        point = group * 16 + z - 128 * i
        placed[0:OUT, 128 * i : 128 * i + 128] = jnp.where(
            lane == point, wide_labels[0], jnp.where(lane == point + 8, wide_labels[1], 0.0)
        )
    placed[OUT:1024, :] = jnp.zeros((1024 - OUT, 256), F32)
    arrived(nys_q)
    blocks = [c * 1024 + ((p + k) % 4) * 256 for k in range(4)]
    nys_own = links.start([(nys(blocks[0], 256), nys(blocks[0], 256), links.core())])
    arrived(swap)

    def other_squares(i, carry):
        rows = pl.ds(pl.multiple_of(1280 + i * 256, 256), 256)
        center_sq[:, pl.ds(pl.multiple_of(1024 + i * 256, 256), 256)] = as_row(
            square_sums(left[rows, :])
        )
        return carry

    lax.fori_loop(0, 4, other_squares, 0)
    arrived(batch_p)
    piece = [nys(blocks[0] + 128 * i, 128) for i in range(2)]
    nys_p = links.start([(piece[0], piece[0], links.along_p(k)) for k in (1, 3)])

    for zz in range(8):
        wide_tiles[zz] = tiles[:, 128 * zz : 128 * zz + 128].astype(F32)
    for zz in range(8):
        for j in range(8):
            wide_batch[j, pl.ds(zz, 32, stride=8), :] = wide_tiles[zz, pl.ds(j, 32, stride=8), :]
    squares = jnp.zeros((256, 128), F32)
    for j in range(8):
        wide = wide_batch[j]
        left[1024:1280, 128 * j : 128 * j + 128] = wide.astype(BF16)
        squares = squares + wide * wide
    left_sq[1024:1280, :] = jnp.sum(squares, axis=1, keepdims=True) * UNIT
    points, points_sq = left[1024:1280, :], left_sq[1024:1280, :]
    for i in range(8):
        first = i * 256 if i < 4 else 256 + i * 256
        k_batch[:, 256 * i : 256 * i + 256] = kernel_values(
            points, points_sq, left[first : first + 256, :], center_sq[:, 256 * i : 256 * i + 256]
        )
    scale = (CEN * 256) ** (-0.5)
    for i in range(4):
        rows = slice(256 * i, 256 * i + 256)
        part[rows, :] = scale * by_rows(rounded[rows, :], k_batch[...]) - placed[rows, :]
    sum_p = links.start(
        [
            (part.at[at(((p + k) % 4) * 256, 256), :], from_p.at[k - 1], links.along_p(k))
            for k in range(1, 4)
        ]
    )
    own_b = at(2048 + c * 256, 256)
    right[own_b, :] = left[1024:1280, :]
    batch_own = links.start([(right.at[own_b, :], right.at[own_b, :], links.core())])

    def fill(first, height):
        cols = pl.ds(pl.multiple_of(first, 256), 256)
        right_sq[:, cols] = as_row(square_sums(right[cols, :]))
        for i in range(2):
            rows = slice(i * (height // 2), (i + 1) * (height // 2))
            table[rows, cols] = kernel_values(
                left[rows, :], left_sq[rows, :], right[cols, :], right_sq[:, cols]
            )

    theirs = [(1 - c) * 1024 + ((q + k) % 4) * 256 for k in range(4)]
    fill(blocks[0], 1280)
    arrived(nys_own)
    fill(theirs[0], 1280)
    fill(2048 + c * 256, 1024)
    arrived(batch_own)
    fill(2304 - c * 256, 1024)

    arrived(sum_p)
    for i in range(4):
        rows = slice(64 * i, 64 * i + 64)
        sum1[rows, :] = (
            part[at(p * 256 + 64 * i, 64), :]
            + from_p[0, rows, :]
            + from_p[1, rows, :]
            + from_p[2, rows, :]
        )
    sum_q = links.start(
        [
            (sum1.at[at(((q + k) % 4) * 64, 64), :], from_q.at[k - 1], links.along_q(k))
            for k in range(1, 4)
        ]
    )
    nys_p += links.start([(piece[1], piece[1], links.along_p(k)) for k in (1, 3)])
    mine = vectors(blocks[0], 256)
    eig_p = links.start([(mine, mine, links.along_p(k)) for k in range(1, 4)])

    arrived(sum_q)
    sum2[...] = sum1[at(q * 64, 64), :] + from_q[0] + from_q[1] + from_q[2]

    def share(ref, first, owner, col=0):
        return ref.at[at(first + (owner // 2) * 16, 16), at(col + (owner % 2) * 128, 128)]

    sum_z = links.start(
        [
            (share(sum2, 0, (z + k) % 8), from_z.at[k - 1], links.along_z(k))
            for k in range(1, 8)
        ]
    )
    nys_far = links.start([(nys(blocks[0], 256), nys(blocks[0], 256), links.along_p(2))])
    arrived(nys_p)
    nys_core = links.start(
        [(nys(blocks[k], 256), nys(blocks[k], 256), links.core()) for k in (1, 3)]
    )
    fill(blocks[1], 1280)
    fill(blocks[3], 1280)

    arrived(sum_z)
    total = share(sum2, 0, z)[...]
    for k in range(7):
        total = total + from_z[k]
    here = at(2048 + c * 256, 256)
    tile = share(coefs, p * 256 + q * 64, z, 2048 + c * 256)
    tile[...] = total.astype(BF16)
    resid_z = links.start([(tile, tile, links.along_z(k)) for k in range(1, 8)])
    arrived(nys_core)
    fill(theirs[1], 1280)
    fill(theirs[3], 1280)
    arrived(eig_p)
    eig_core = links.start([(vectors(c * 1024, 1024), vectors(c * 1024, 1024), links.core())])

    arrived(resid_z)
    tile = coefs.at[at(p * 256 + q * 64, 64), here]
    resid_q = links.start([(tile, tile, links.along_q(k)) for k in range(1, 4)])
    arrived(nys_far)
    nys_last = links.start([(nys(blocks[2], 256), nys(blocks[2], 256), links.core())])
    fill(blocks[2], 1280)
    arrived(eig_core)

    narrow = lax.broadcasted_iota(jnp.int32, (256, 128), 1) < 32

    def split(i, carry):
        rows = at(i * 256, 256)
        some = eig[pl.ds(i * 8, 8), :, :]
        high, middle, low = three(some[:, 0:32, :].reshape(256, 128))
        stack[rows, 0:128] = high
        stack[rows, 128:256] = high
        stack[rows, 256:384] = middle
        stack[rows, 512:640] = low
        rest = some[:, 32:40, :].reshape(64, 128)
        rest = [rest] + [pltpu.roll(rest, 128 - 32 * k, 1) for k in range(1, 4)]
        rest = jnp.concatenate([v.reshape(8, 8, 128) for v in rest], axis=1).reshape(256, 128)
        high, middle, low = three(jnp.where(narrow, rest, 0.0))
        stack[rows, 384:512] = beside(high, high, middle)
        stack[rows, 640:768] = low
        return carry

    lax.fori_loop(0, 8, split, 0)
    arrived(resid_q)
    tile = coefs.at[at(p * 256, 256), here]
    resid_p = links.start([(tile, tile, links.along_p(k)) for k in range(1, 4)])
    resid_core = links.start([(tile, tile, links.core())])
    arrived(nys_last)
    fill(theirs[2], 1280)

    loads[6].wait()
    product = jnp.dot(table[1024:1280, 0:NYS], stack[...], preferred_element_type=F32)
    value = product[:, 0:128] + product[:, 256:384] + product[:, 512:640]
    high, middle, low = three(value * small_corr[:, 0:128])
    rows = at(c * 256, 256)
    mixed[rows, 0:128] = high
    mixed[rows, 128:256] = middle
    mixed[rows, 256:384] = low
    value = product[:, 384:512]
    value = value + pltpu.roll(value, 64, 1) + product[:, 640:768]
    high, middle, low = three(jnp.where(narrow, value * small_corr[:, 128:256], 0.0))
    mixed[rows, 384:512] = beside(high, middle, low)
    mixed_core = links.start([(mixed.at[rows, :], mixed.at[rows, :], links.core())])
    for k, copy in zip((1, 2, 3), resid_p):
        arrived([copy])
        tile = coefs.at[at(((p + 4 - k) % 4) * 256, 256), here]
        resid_core += links.start([(tile, tile, links.core())])
    arrived(mixed_core)
    arrived(resid_core)

    narrow = lax.broadcasted_iota(jnp.int32, (1024, 128), 1) < 32
    value = jnp.dot(coefs[:, 2048:2560], mixed[...], preferred_element_type=F32)
    high, middle, _ = three(value[:, 0:128] + value[:, 128:256] + value[:, 256:384])
    scaled[:, 0:128] = high
    scaled[:, 128:256] = middle
    scaled[:, 256:384] = high
    value = value[:, 384:512]
    value = value + pltpu.roll(value, 96, 1) + pltpu.roll(value, 64, 1)
    high, middle, _ = three(jnp.where(narrow, value, 0.0))
    scaled[:, 384:512] = beside(high, middle, high)
    for i in range(4):
        cols = slice(512 * i, 512 * i + 512)
        for k in range(2):
            rows = slice(512 * k, 512 * k + 512)
            coefs[rows, cols] = (-by_rows(scaled[rows, :], stack[cols, 0:512])).astype(BF16)
    for i in range(4):
        cols = slice(256 * i, 256 * i + 256)
        for rows in (slice(0, 512), slice(512, OUT)):
            change = by_rows(coefs[rows.start : rows.start + 512, :], table[cols, :])
            out[rows, cols] = old[rows, cols] - (RATE / BATCH) * change[0 : rows.stop - rows.start]
    for copy in links.all:
        copy.wait_send()


def by_rows(a, b):
    return lax.dot_general(a, b, (((1,), (1,)), ((), ())), preferred_element_type=F32)


def beside(a, b, c):
    a, b, c = (v.astype(F32) for v in (a, b, c))
    return (a + pltpu.roll(b, 32, 1) + pltpu.roll(c, 64, 1)).astype(BF16)


def per_device(centers, weights, batch_points, labels, nystrom_points, eigvecs, corrections):
    anywhere = pl.BlockSpec(memory_space=pl.ANY)
    vmem = pltpu.VMEM
    return pl.pallas_call(
        step_kernel,
        out_shape=jax.ShapeDtypeStruct((OUT, CEN), F32),
        in_specs=[anywhere] * 7,
        out_specs=pl.BlockSpec(memory_space=vmem),
        scratch_shapes=[
            vmem((2304, FEATURES), BF16),
            vmem((1280, 1), F32),
            vmem((2560, FEATURES), BF16),
            vmem((1, 2560), F32),
            vmem((1, 2048), F32),
            vmem((2, FEATURES), BF16),
            vmem((2, OUT), F32),
            vmem((64, Q), F32),
            vmem((1, 256), F32),
            vmem((256, FEATURES), BF16),
            vmem((8, 256, 128), F32),
            vmem((8, 256, 128), F32),
            vmem((OUT, CEN), F32),
            vmem((1024, 2048), BF16),
            vmem((64, 40, 128), F32),
            vmem((NYS, 768), BF16),
            vmem((256, 2048), BF16),
            vmem((1024, 256), F32),
            vmem((1024, 256), F32),
            vmem((256, 256), F32),
            vmem((64, 256), F32),
            vmem((3, 256, 256), F32),
            vmem((3, 64, 256), F32),
            vmem((7, 16, 128), F32),
            vmem((1280, 2560), BF16),
            vmem((BATCH, 512), BF16),
            vmem((1024, 2560), BF16),
            vmem((1024, 512), BF16),
            pltpu.SemaphoreType.DMA((80,)),
            pltpu.SemaphoreType.DMA((80,)),
            pltpu.SemaphoreType.DMA((7,)),
        ],
        compiler_params=pltpu.CompilerParams(
            collective_id=0, has_side_effects=True, vmem_limit_bytes=60 << 20
        ),
        name="step",
    )(
        centers,
        weights.T,
        batch_points,
        labels,
        nystrom_points,
        eigvecs,
        jnp.pad(corrections, (0, 256 - Q)).reshape(1, 256),
    ).T


def solution(mesh):
    every = P(("narrow", "wide", "nys"), None)
    some = P(("narrow", "nys"), None)
    return jax.shard_map(
        per_device,
        mesh=mesh,
        in_specs=(every, every, every, every, some, some, P()),
        out_specs=every,
        check_vma=False,
    )
```

```python
import math

import jax
import jax.numpy as jnp
from jax import lax
from jax.experimental import pallas as pl
from jax.experimental.pallas import tpu as pltpu
from jax.sharding import PartitionSpec as P

RATE = 16.0
SPREAD = 4.0
MESH = pl.DeviceIdType.MESH
F32, BF16 = jnp.float32, jnp.bfloat16

FEATURES = 1024
CEN = 1024
OUT = 1000
NYS = 2048
BATCH = 512
Q = 160
UNIT = (math.log2(math.e) / SPREAD) ** 2
TOP = math.sqrt(2.0 * FEATURES) * math.log2(math.e) / SPREAD


def device(x, y, z, c):
    return (y * 2 + z % 2, (z // 2) * 2 + c, x)


class Links:
    def __init__(self, send, recv):
        n, w, self.x = (lax.axis_index(a) for a in ("narrow", "wide", "nys"))
        self.y, self.c = n // 2, w % 2
        self.z = (w // 2) * 2 + n % 2
        self.p = self.x * (1 - self.c) + self.y * self.c
        self.q = self.y * (1 - self.c) + self.x * self.c
        self.send, self.recv, self.next, self.all = send, recv, 0, []

    def core(self):
        return device(self.x, self.y, self.z, 1 - self.c)

    def along_p(self, k):
        c = self.c
        return device((self.x + k * (1 - c)) % 4, (self.y + k * c) % 4, self.z, c)

    def along_q(self, k):
        c = self.c
        return device((self.x + k * c) % 4, (self.y + k * (1 - c)) % 4, self.z, c)

    def along_z(self, k):
        return device(self.x, self.y, (self.z + k) % 8, self.c)

    def z_pair(self):
        return device(self.x, self.y, self.z + 1 - 2 * (self.z % 2), self.c)

    def peers(self):
        out = [self.core()]
        out += [self.along_p(k) for k in range(1, 4)]
        out += [self.along_q(k) for k in range(1, 4)]
        out += [self.along_z(k) for k in range(1, 8)]
        return out

    def start(self, pairs):
        out = []
        for src, dst, peer in pairs:
            copy = pltpu.make_async_remote_copy(
                src_ref=src,
                dst_ref=dst,
                send_sem=self.send.at[self.next],
                recv_sem=self.recv.at[self.next],
                device_id=peer,
                device_id_type=MESH,
            )
            self.next += 1
            copy.start()
            out.append(copy)
        self.all += out
        return out


def arrived(copies):
    for copy in copies:
        copy.wait_recv()


def at(start, size, unit=None):
    if isinstance(start, int):
        return slice(start, start + size)
    return pl.ds(pl.multiple_of(start, unit or size), size)


def square_sums(points):
    wide = points.astype(F32)
    return jnp.sum(wide * wide, axis=1, keepdims=True) * UNIT


def as_row(column):
    return jnp.transpose(jnp.broadcast_to(column, (column.shape[0], 128)))[0:1, :]


def kernel_values(left, left_sq, right, right_sq):
    cross = lax.dot_general(left, right, (((1,), (1,)), ((), ())), preferred_element_type=F32)
    dist_sq = jnp.maximum((left_sq + right_sq) - (2.0 * UNIT) * cross, 1e-30)
    return jnp.exp2(TOP - dist_sq * lax.rsqrt(dist_sq)).astype(BF16)


def three(value):
    high = value.astype(BF16)
    rest = value - high.astype(F32)
    middle = rest.astype(BF16)
    low = (rest - middle.astype(F32)).astype(BF16)
    return high, middle, low


def step_kernel(
    centers,
    weights,
    batch,
    labels,
    nystrom,
    eigvecs,
    corrections,
    out,
    left,
    left_sq,
    right,
    right_sq,
    center_sq,
    small_batch,
    small_labels,
    small_eig,
    small_corr,
    wide_corr,
    tiles,
    wide_tiles,
    wide_batch,
    old,
    rounded,
    eig,
    stack,
    k_batch,
    part,
    placed,
    sum1,
    sum2,
    from_p,
    from_q,
    from_z,
    gathered,
    table,
    mixed,
    coefs,
    scaled,
    send,
    recv,
    local,
):
    links = Links(send, recv)
    c, p, q, z = links.c, links.p, links.q, links.z
    group = p * 4 + q

    own_n = c * 1024 + p * 256 + q * 64 + (z % 2) * 32
    loads = [
        (batch, small_batch),
        (labels, small_labels),
        (eigvecs, small_eig),
        (nystrom.at[at(c * 32, 32), :], right.at[at(own_n, 32), :]),
        (centers, left.at[0:1024, :]),
        (weights, old),
        (corrections, small_corr),
    ]
    loads = [pltpu.make_async_copy(s, d, local.at[i]) for i, (s, d) in enumerate(loads)]
    for load in loads:
        load.start()
    barrier = pltpu.get_barrier_semaphore()
    peers = links.peers()
    for peer in peers:
        pl.semaphore_signal(barrier, inc=1, device_id=peer, device_id_type=MESH)

    loads[0].wait()
    pair = small_batch[...].astype(F32)
    for r in range(2):
        for j in range(8):
            wide_tiles[0, 8 * r + j : 8 * r + j + 1, :] = pair[r : r + 1, 128 * j : 128 * j + 128]
    tiles[at(group * 16, 16), at(z * 128, 128)] = wide_tiles[0, 0:16, :].astype(BF16)
    loads[2].wait()
    own_e = own_n // 32
    mine = small_eig[at(c * 32, 32), :]
    eig[own_e, 0:32, :] = mine[:, 0:128]
    for k in range(4):
        eig[own_e, 32:40, 32 * k : 32 * k + 32] = mine[8 * k : 8 * k + 8, 128:Q]
    loads[3].wait()
    pl.semaphore_wait(barrier, len(peers))

    def nys(first, count):
        return right.at[at(first, count, count), :]

    def vectors(first, count):
        return eig.at[pl.ds(first // 32, count // 32)]

    tile = tiles.at[at(group * 16, 16), at(z * 128, 128)]
    batch_q = links.start([(tile, tile, links.along_q(k)) for k in range(1, 4)])
    own = [nys(own_n, 32), vectors(own_n, 32)]
    nys_z = links.start([(o, o, links.z_pair()) for o in own])
    loads[4].wait()
    swap = links.start([(left.at[0:1024, :], left.at[1280:2304, :], links.core())])

    arrived(batch_q)
    tile = tiles.at[at(p * 64, 64), at(z * 128, 128)]
    batch_z = links.start([(tile, tile, links.along_z(k)) for k in range(1, 8)])
    arrived(nys_z)
    own_q = c * 1024 + p * 256 + q * 64
    own = [nys(own_q, 64), vectors(own_q, 64)]
    nys_q = links.start([(o, o, links.along_q(k)) for k in range(1, 4) for o in own])

    loads[5].wait()
    for i in range(7):
        rows = slice(128 * i, 128 * i + 128)
        rounded[rows, 0:1024] = old[rows, :].astype(BF16)
    last = jnp.concatenate([old[896:OUT, :], jnp.zeros((1024 - OUT, CEN), F32)], axis=0)
    rounded[896:1024, 0:1024] = last.astype(BF16)
    swap += links.start([(rounded.at[:, 0:1024], rounded.at[:, 1024:2048], links.core())])

    arrived(batch_z)
    block = tiles.at[at(p * 64, 64), :]
    batch_p = links.start([(block, block, links.along_p(k)) for k in range(1, 4)])

    def own_squares(i, carry):
        rows = at(i * 256, 256)
        value = square_sums(left[rows, :])
        left_sq[rows, :] = value
        center_sq[:, rows] = as_row(value)
        return carry

    lax.fori_loop(0, 4, own_squares, 0)
    loads[1].wait()
    wide_labels = [
        jnp.transpose(jnp.broadcast_to(small_labels[r : r + 1, :], (128, OUT))) for r in range(2)
    ]
    lane = lax.broadcasted_iota(jnp.int32, (OUT, 128), 1)
    for i in range(2):
        point = group * 16 + z - 128 * i
        placed[0:OUT, 128 * i : 128 * i + 128] = jnp.where(
            lane == point, wide_labels[0], jnp.where(lane == point + 8, wide_labels[1], 0.0)
        )
    placed[OUT:1024, :] = jnp.zeros((1024 - OUT, 256), F32)
    arrived(nys_q)
    blocks = [c * 1024 + ((p + k) % 4) * 256 for k in range(4)]
    nys_own = links.start([(nys(blocks[0], 256), nys(blocks[0], 256), links.core())])
    arrived(swap)

    def other_squares(i, carry):
        rows = pl.ds(pl.multiple_of(1280 + i * 256, 256), 256)
        center_sq[:, pl.ds(pl.multiple_of(1024 + i * 256, 256), 256)] = as_row(
            square_sums(left[rows, :])
        )
        return carry

    lax.fori_loop(0, 4, other_squares, 0)
    arrived(batch_p)
    piece = [nys(blocks[0] + 128 * i, 128) for i in range(2)]
    nys_p = links.start([(piece[0], piece[0], links.along_p(k)) for k in (1, 3)])

    for zz in range(8):
        wide_tiles[zz] = tiles[:, 128 * zz : 128 * zz + 128].astype(F32)
    for zz in range(8):
        for j in range(8):
            wide_batch[j, pl.ds(zz, 32, stride=8), :] = wide_tiles[zz, pl.ds(j, 32, stride=8), :]
    squares = jnp.zeros((256, 128), F32)
    for j in range(8):
        wide = wide_batch[j]
        left[1024:1280, 128 * j : 128 * j + 128] = wide.astype(BF16)
        squares = squares + wide * wide
    left_sq[1024:1280, :] = jnp.sum(squares, axis=1, keepdims=True) * UNIT
    points, points_sq = left[1024:1280, :], left_sq[1024:1280, :]
    for i in range(8):
        first = i * 256 if i < 4 else 256 + i * 256
        k_batch[:, 256 * i : 256 * i + 256] = kernel_values(
            points, points_sq, left[first : first + 256, :], center_sq[:, 256 * i : 256 * i + 256]
        )
    scale = (CEN * 256) ** (-0.5)
    sum_p = []
    for h in range(2):
        for i in range(2):
            rows = slice(512 * h + 256 * i, 512 * h + 256 * i + 256)
            part[rows, :] = scale * by_rows(rounded[rows, :], k_batch[...]) - placed[rows, :]
        sum_p.append(
            links.start(
                [
                    (
                        part.at[at(512 * h + ((p + k) % 4) * 128, 128), :],
                        from_p.at[h, k - 1],
                        links.along_p(k),
                    )
                    for k in range(1, 4)
                ]
            )
        )
    own_b = at(2048 + c * 256, 256)
    right[own_b, :] = left[1024:1280, :]
    batch_own = links.start([(right.at[own_b, :], right.at[own_b, :], links.core())])

    def fill(first, height):
        cols = pl.ds(pl.multiple_of(first, 256), 256)
        right_sq[:, cols] = as_row(square_sums(right[cols, :]))
        for i in range(2):
            rows = slice(i * (height // 2), (i + 1) * (height // 2))
            table[rows, cols] = kernel_values(
                left[rows, :], left_sq[rows, :], right[cols, :], right_sq[:, cols]
            )

    theirs = [(1 - c) * 1024 + ((q + k) % 4) * 256 for k in range(4)]
    here = at(2048 + c * 256, 256)

    def start_sum_q(h):
        arrived(sum_p[h])
        for i in range(2):
            rows = slice(64 * i, 64 * i + 64)
            sum1[h, rows, :] = (
                part[at(512 * h + p * 128 + 64 * i, 64), :]
                + from_p[h, 0, rows, :]
                + from_p[h, 1, rows, :]
                + from_p[h, 2, rows, :]
            )
        return links.start(
            [
                (
                    sum1.at[h, at(((q + k) % 4) * 32, 32), :],
                    from_q.at[h, k - 1],
                    links.along_q(k),
                )
                for k in range(1, 4)
            ]
        )

    def share(h, owner):
        return sum2.at[h, at((owner // 2) * 8, 8), at((owner % 2) * 128, 128)]

    def start_sum_z(h):
        arrived(sum_q[h])
        sum2[h] = sum1[h, at(q * 32, 32), :] + from_q[h, 0] + from_q[h, 1] + from_q[h, 2]
        return links.start(
            [
                (share(h, (z + k) % 8), from_z.at[h, k - 1], links.along_z(k))
                for k in range(1, 8)
            ]
        )

    def start_resid_z(h):
        arrived(sum_z[h])
        total = share(h, z)[...]
        for k in range(7):
            total = total + from_z[h, k]
        gathered[h, z] = total
        tile = gathered.at[h, z]
        return links.start([(tile, tile, links.along_z(k)) for k in range(1, 8)])

    def resid_rows(h, first, count):
        return coefs.at[at(512 * h + first, count), here]

    def start_resid_q(h):
        arrived(resid_z[h])
        rows = [
            jnp.concatenate([gathered[h, 2 * i], gathered[h, 2 * i + 1]], axis=1) for i in range(4)
        ]
        tile = resid_rows(h, p * 128 + q * 32, 32)
        tile[...] = jnp.concatenate(rows, axis=0).astype(BF16)
        return links.start([(tile, tile, links.along_q(k)) for k in range(1, 4)])

    def start_resid_p(h):
        arrived(resid_q[h])
        tile = resid_rows(h, p * 128, 128)
        out = links.start([(tile, tile, links.along_p(k)) for k in range(1, 4)])
        return out, links.start([(tile, tile, links.core())])

    def pass_on(h):
        copies, more = resid_p[h]
        for k, copy in zip((1, 2, 3), copies):
            arrived([copy])
            tile = resid_rows(h, ((p + 4 - k) % 4) * 128, 128)
            more += links.start([(tile, tile, links.core())])
        return more

    fill(blocks[0], 1280)
    arrived(nys_own)
    fill(theirs[0], 1280)
    sum_q = [start_sum_q(0)]
    fill(2048 + c * 256, 1024)
    sum_q.append(start_sum_q(1))
    nys_p += links.start([(piece[1], piece[1], links.along_p(k)) for k in (1, 3)])
    mine = vectors(blocks[0], 256)
    eig_p = links.start([(mine, mine, links.along_p(k)) for k in range(1, 4)])
    arrived(batch_own)
    fill(2304 - c * 256, 1024)
    sum_z = [start_sum_z(0)]
    sum_z.append(start_sum_z(1))
    nys_far = links.start([(nys(blocks[0], 256), nys(blocks[0], 256), links.along_p(2))])
    resid_z = [start_resid_z(0)]
    resid_z.append(start_resid_z(1))
    arrived(nys_p)
    nys_core = links.start(
        [(nys(blocks[k], 256), nys(blocks[k], 256), links.core()) for k in (1, 3)]
    )
    fill(blocks[1], 1280)
    fill(blocks[3], 1280)
    arrived(nys_core)
    fill(theirs[1], 1280)
    fill(theirs[3], 1280)
    resid_q = [start_resid_q(0)]
    resid_q.append(start_resid_q(1))
    arrived(eig_p)
    eig_core = links.start([(vectors(c * 1024, 1024), vectors(c * 1024, 1024), links.core())])
    arrived(nys_far)
    nys_last = links.start([(nys(blocks[2], 256), nys(blocks[2], 256), links.core())])
    fill(blocks[2], 1280)
    resid_p = [start_resid_p(0)]
    resid_p.append(start_resid_p(1))
    arrived(eig_core)

    narrow = lax.broadcasted_iota(jnp.int32, (256, 128), 1) < 32

    def split(i, carry):
        rows = at(i * 256, 256)
        some = eig[pl.ds(i * 8, 8), :, :]
        high, middle, low = three(some[:, 0:32, :].reshape(256, 128))
        stack[rows, 0:128] = high
        stack[rows, 128:256] = high
        stack[rows, 256:384] = middle
        stack[rows, 512:640] = low
        rest = some[:, 32:40, :].reshape(64, 128)
        rest = [rest] + [pltpu.roll(rest, 128 - 32 * k, 1) for k in range(1, 4)]
        rest = jnp.concatenate([v.reshape(8, 8, 128) for v in rest], axis=1).reshape(256, 128)
        high, middle, low = three(jnp.where(narrow, rest, 0.0))
        stack[rows, 384:512] = beside(high, high, middle)
        stack[rows, 640:768] = low
        return carry

    lax.fori_loop(0, 8, split, 0)
    arrived(nys_last)
    fill(theirs[2], 1280)

    loads[6].wait()
    wide_corr[...] = jnp.zeros((1, 256), F32)
    wide_corr[:, 0:Q] = small_corr[...]
    product = jnp.dot(table[1024:1280, 0:NYS], stack[...], preferred_element_type=F32)
    value = product[:, 0:128] + product[:, 256:384] + product[:, 512:640]
    high, middle, low = three(value * wide_corr[:, 0:128])
    rows = at(c * 256, 256)
    mixed[rows, 0:128] = high
    mixed[rows, 128:256] = middle
    mixed[rows, 256:384] = low
    value = product[:, 384:512]
    value = value + pltpu.roll(value, 64, 1) + product[:, 640:768]
    high, middle, low = three(jnp.where(narrow, value * wide_corr[:, 128:256], 0.0))
    mixed[rows, 384:512] = beside(high, middle, low)
    mixed_core = links.start([(mixed.at[rows, :], mixed.at[rows, :], links.core())])
    narrow = lax.broadcasted_iota(jnp.int32, (512, 128), 1) < 32

    def project(h):
        rows = slice(512 * h, 512 * h + 512)
        value = jnp.dot(coefs[rows, 2048:2560], mixed[...], preferred_element_type=F32)
        high, middle, _ = three(value[:, 0:128] + value[:, 128:256] + value[:, 256:384])
        scaled[rows, 0:128] = high
        scaled[rows, 128:256] = middle
        scaled[rows, 256:384] = high
        value = value[:, 384:512]
        value = value + pltpu.roll(value, 96, 1) + pltpu.roll(value, 64, 1)
        high, middle, _ = three(jnp.where(narrow, value, 0.0))
        scaled[rows, 384:512] = beside(high, middle, high)

    def finish(h):
        rows = slice(512 * h, 512 * h + 512)
        for i in range(4):
            cols = slice(512 * i, 512 * i + 512)
            coefs[rows, cols] = (-by_rows(scaled[rows, :], stack[cols, 0:512])).astype(BF16)
        kept = min(512, OUT - 512 * h)
        for i in range(4):
            cols = slice(256 * i, 256 * i + 256)
            change = by_rows(coefs[rows, :], table[cols, :])
            out[512 * h : 512 * h + kept, cols] = (RATE / BATCH) * change[0:kept]

    resid_core = pass_on(0)
    arrived(mixed_core)
    arrived(resid_core)
    project(0)
    resid_core = pass_on(1)
    finish(0)
    arrived(resid_core)
    project(1)
    finish(1)
    for copy in links.all:
        copy.wait_send()


def by_rows(a, b):
    return lax.dot_general(a, b, (((1,), (1,)), ((), ())), preferred_element_type=F32)


def beside(a, b, c):
    a, b, c = (v.astype(F32) for v in (a, b, c))
    return (a + pltpu.roll(b, 32, 1) + pltpu.roll(c, 64, 1)).astype(BF16)


def per_device(centers, weights, batch_points, labels, nystrom_points, eigvecs, corrections):
    hbm = pl.BlockSpec(memory_space=pltpu.HBM)
    vmem = pltpu.VMEM
    change = pl.pallas_call(
        step_kernel,
        out_shape=jax.ShapeDtypeStruct((OUT, CEN), F32),
        in_specs=[hbm] * 7,
        out_specs=pl.BlockSpec(memory_space=vmem),
        scratch_shapes=[
            vmem((2304, FEATURES), BF16),
            vmem((1280, 1), F32),
            vmem((2560, FEATURES), BF16),
            vmem((1, 2560), F32),
            vmem((1, 2048), F32),
            vmem((2, FEATURES), BF16),
            vmem((2, OUT), F32),
            vmem((64, Q), F32),
            vmem((1, Q), F32),
            vmem((1, 256), F32),
            vmem((256, FEATURES), BF16),
            vmem((8, 256, 128), F32),
            vmem((8, 256, 128), F32),
            vmem((OUT, CEN), F32),
            vmem((1024, 2048), BF16),
            vmem((64, 40, 128), F32),
            vmem((NYS, 768), BF16),
            vmem((256, 2048), BF16),
            vmem((1024, 256), F32),
            vmem((1024, 256), F32),
            vmem((2, 128, 256), F32),
            vmem((2, 32, 256), F32),
            vmem((2, 3, 128, 256), F32),
            vmem((2, 3, 32, 256), F32),
            vmem((2, 7, 8, 128), F32),
            vmem((2, 8, 8, 128), F32),
            vmem((1280, 2560), BF16),
            vmem((BATCH, 512), BF16),
            vmem((1024, 2560), BF16),
            vmem((1024, 512), BF16),
            pltpu.SemaphoreType.DMA((110,)),
            pltpu.SemaphoreType.DMA((110,)),
            pltpu.SemaphoreType.DMA((7,)),
        ],
        compiler_params=pltpu.CompilerParams(
            collective_id=0, has_side_effects=True, vmem_limit_bytes=50 << 20
        ),
        name="step",
    )(
        *(
            pltpu.with_memory_space_constraint(v, pltpu.HBM)
            for v in (
                centers,
                weights.T,
                batch_points,
                labels,
                nystrom_points,
                eigvecs,
                corrections.reshape(1, Q),
            )
        )
    )
    return (weights.T - change).T


def solution(mesh):
    every = P(("narrow", "wide", "nys"), None)
    some = P(("narrow", "nys"), None)
    return jax.shard_map(
        per_device,
        mesh=mesh,
        in_specs=(every, every, every, every, some, some, P()),
        out_specs=every,
        check_vma=False,
    )
```

```python
import math

import jax
import jax.numpy as jnp
from jax import lax
from jax.experimental import pallas as pl
from jax.experimental.pallas import tpu as pltpu
from jax.sharding import PartitionSpec as P

RATE = 16.0
SPREAD = 4.0
MESH = pl.DeviceIdType.MESH
F32, BF16 = jnp.float32, jnp.bfloat16

FEATURES = 1024
CEN = 1024
OUT = 1000
NYS = 2048
BATCH = 512
Q = 160
UNIT = (math.log2(math.e) / SPREAD) ** 2
TOP = math.sqrt(2.0 * FEATURES) * math.log2(math.e) / SPREAD


def device(x, y, z, c):
    return (y * 2 + z % 2, (z // 2) * 2 + c, x)


class Links:
    def __init__(self, send, recv):
        n, w, self.x = (lax.axis_index(a) for a in ("narrow", "wide", "nys"))
        self.y, self.c = n // 2, w % 2
        self.z = (w // 2) * 2 + n % 2
        self.p = self.x * (1 - self.c) + self.y * self.c
        self.q = self.y * (1 - self.c) + self.x * self.c
        self.send, self.recv, self.next, self.all = send, recv, 0, []

    def core(self):
        return device(self.x, self.y, self.z, 1 - self.c)

    def along_p(self, k):
        c = self.c
        return device((self.x + k * (1 - c)) % 4, (self.y + k * c) % 4, self.z, c)

    def along_q(self, k):
        c = self.c
        return device((self.x + k * c) % 4, (self.y + k * (1 - c)) % 4, self.z, c)

    def along_z(self, k):
        return device(self.x, self.y, (self.z + k) % 8, self.c)

    def z_pair(self):
        return device(self.x, self.y, self.z + 1 - 2 * (self.z % 2), self.c)

    def peers(self):
        out = [self.core()]
        out += [self.along_p(k) for k in range(1, 4)]
        out += [self.along_q(k) for k in range(1, 4)]
        out += [self.along_z(k) for k in range(1, 8)]
        return out

    def start(self, pairs):
        out = []
        for src, dst, peer in pairs:
            copy = pltpu.make_async_remote_copy(
                src_ref=src,
                dst_ref=dst,
                send_sem=self.send.at[self.next],
                recv_sem=self.recv.at[self.next],
                device_id=peer,
                device_id_type=MESH,
            )
            self.next += 1
            copy.start()
            out.append(copy)
        self.all += out
        return out


def arrived(copies):
    for copy in copies:
        copy.wait_recv()


def at(start, size, unit=None):
    if isinstance(start, int):
        return slice(start, start + size)
    return pl.ds(pl.multiple_of(start, unit or size), size)


def square_sums(points):
    wide = points.astype(F32)
    return jnp.sum(wide * wide, axis=1, keepdims=True) * UNIT


def as_row(column):
    return jnp.transpose(jnp.broadcast_to(column, (column.shape[0], 128)))[0:1, :]


def kernel_values(left, left_sq, right, right_sq):
    cross = lax.dot_general(left, right, (((1,), (1,)), ((), ())), preferred_element_type=F32)
    dist_sq = jnp.maximum((left_sq + right_sq) - (2.0 * UNIT) * cross, 1e-30)
    return jnp.exp2(TOP - dist_sq * lax.rsqrt(dist_sq)).astype(BF16)


def three(value):
    high = value.astype(BF16)
    rest = value - high.astype(F32)
    middle = rest.astype(BF16)
    low = (rest - middle.astype(F32)).astype(BF16)
    return high, middle, low


def step_kernel(
    centers,
    weights,
    batch,
    labels,
    nystrom,
    eigvecs,
    corrections,
    stack,
    table,
    mixed,
    resid,
    left,
    left_sq,
    right,
    right_sq,
    center_sq,
    small_batch,
    small_labels,
    small_eig,
    small_corr,
    wide_corr,
    tiles,
    wide_tiles,
    wide_batch,
    old,
    rounded,
    eig,
    k_batch,
    part,
    placed,
    sum1,
    sum2,
    from_p,
    from_q,
    from_z,
    gathered,
    send,
    recv,
    local,
):
    links = Links(send, recv)
    c, p, q, z = links.c, links.p, links.q, links.z
    group = p * 4 + q

    own_n = c * 1024 + p * 256 + (z % 2) * 128 + q * 32
    loads = [
        (batch, small_batch),
        (labels, small_labels),
        (eigvecs, small_eig),
        (nystrom.at[at(c * 32, 32), :], right.at[at(own_n, 32), :]),
        (centers, left.at[0:1024, :]),
        (weights, old),
        (corrections, small_corr),
    ]
    loads = [pltpu.make_async_copy(s, d, local.at[i]) for i, (s, d) in enumerate(loads)]
    for load in loads:
        load.start()
    barrier = pltpu.get_barrier_semaphore()
    peers = links.peers()
    for peer in peers:
        pl.semaphore_signal(barrier, inc=1, device_id=peer, device_id_type=MESH)

    loads[0].wait()
    pair = small_batch[...].astype(F32)
    for r in range(2):
        for j in range(8):
            wide_tiles[0, 8 * r + j : 8 * r + j + 1, :] = pair[r : r + 1, 128 * j : 128 * j + 128]
    tiles[at(group * 16, 16), at(z * 128, 128)] = wide_tiles[0, 0:16, :].astype(BF16)
    loads[2].wait()
    own_e = own_n // 32
    mine = small_eig[at(c * 32, 32), :]
    eig[own_e, 0:32, :] = mine[:, 0:128]
    for k in range(4):
        eig[own_e, 32:40, 32 * k : 32 * k + 32] = mine[8 * k : 8 * k + 8, 128:Q]
    loads[3].wait()
    pl.semaphore_wait(barrier, len(peers))

    def nys(first, count):
        return right.at[at(first, count, count), :]

    def vectors(first, count):
        return eig.at[pl.ds(first // 32, count // 32)]

    tile = tiles.at[at(group * 16, 16), at(z * 128, 128)]
    batch_z = links.start([(tile, tile, links.along_z(k)) for k in range(1, 8)])
    own = [nys(own_n, 32), vectors(own_n, 32)]
    nys_q = links.start([(o, o, links.along_q(k)) for k in range(1, 4) for o in own])
    loads[4].wait()
    swap = links.start([(left.at[0:1024, :], left.at[1280:2304, :], links.core())])

    arrived(batch_z)
    tile = tiles.at[at(group * 16, 16), :]
    batch_q = links.start([(tile, tile, links.along_q(k)) for k in range(1, 4)])
    arrived(nys_q)
    own_z = c * 1024 + p * 256 + (z % 2) * 128
    own = [nys(own_z, 128), vectors(own_z, 128)]
    nys_z = links.start([(o, o, links.z_pair()) for o in own])

    loads[5].wait()
    for i in range(7):
        rows = slice(128 * i, 128 * i + 128)
        rounded[rows, 0:1024] = old[rows, :].astype(BF16)
    last = jnp.concatenate([old[896:OUT, :], jnp.zeros((1024 - OUT, CEN), F32)], axis=0)
    rounded[896:1024, 0:1024] = last.astype(BF16)
    swap += links.start([(rounded.at[:, 0:1024], rounded.at[:, 1024:2048], links.core())])

    arrived(batch_q)
    block = tiles.at[at(p * 64, 64), :]
    batch_p = links.start([(block, block, links.along_p(k)) for k in range(1, 4)])

    def own_squares(i, carry):
        rows = at(i * 256, 256)
        value = square_sums(left[rows, :])
        left_sq[rows, :] = value
        center_sq[:, rows] = as_row(value)
        return carry

    lax.fori_loop(0, 4, own_squares, 0)
    loads[1].wait()
    wide_labels = [
        jnp.transpose(jnp.broadcast_to(small_labels[r : r + 1, :], (128, OUT))) for r in range(2)
    ]
    lane = lax.broadcasted_iota(jnp.int32, (OUT, 128), 1)
    for i in range(2):
        point = group * 16 + z - 128 * i
        placed[0:OUT, 128 * i : 128 * i + 128] = jnp.where(
            lane == point, wide_labels[0], jnp.where(lane == point + 8, wide_labels[1], 0.0)
        )
    placed[OUT:1024, :] = jnp.zeros((1024 - OUT, 256), F32)
    blocks = [c * 1024 + ((p + k) % 4) * 256 for k in range(4)]
    arrived(swap)

    def other_squares(i, carry):
        rows = pl.ds(pl.multiple_of(1280 + i * 256, 256), 256)
        center_sq[:, pl.ds(pl.multiple_of(1024 + i * 256, 256), 256)] = as_row(
            square_sums(left[rows, :])
        )
        return carry

    lax.fori_loop(0, 4, other_squares, 0)
    arrived(batch_p)
    arrived(nys_z)
    nys_own = links.start([(nys(blocks[0], 256), nys(blocks[0], 256), links.core())])
    piece = [nys(blocks[0] + 128 * i, 128) for i in range(2)]
    nys_p = links.start([(piece[0], piece[0], links.along_p(k)) for k in (1, 3)])

    for zz in range(8):
        wide_tiles[zz] = tiles[:, 128 * zz : 128 * zz + 128].astype(F32)
    for zz in range(8):
        for j in range(8):
            wide_batch[j, pl.ds(zz, 32, stride=8), :] = wide_tiles[zz, pl.ds(j, 32, stride=8), :]
    squares = jnp.zeros((256, 128), F32)
    for j in range(8):
        wide = wide_batch[j]
        left[1024:1280, 128 * j : 128 * j + 128] = wide.astype(BF16)
        squares = squares + wide * wide
    left_sq[1024:1280, :] = jnp.sum(squares, axis=1, keepdims=True) * UNIT
    points, points_sq = left[1024:1280, :], left_sq[1024:1280, :]
    for i in range(8):
        first = i * 256 if i < 4 else 256 + i * 256
        k_batch[:, 256 * i : 256 * i + 256] = kernel_values(
            points, points_sq, left[first : first + 256, :], center_sq[:, 256 * i : 256 * i + 256]
        )
    scale = (CEN * 256) ** (-0.5)
    sum_p = []
    for h in range(2):
        for i in range(2):
            rows = slice(512 * h + 256 * i, 512 * h + 256 * i + 256)
            part[rows, :] = scale * by_rows(rounded[rows, :], k_batch[...]) - placed[rows, :]
        sum_p.append(
            links.start(
                [
                    (
                        part.at[at(512 * h + ((p + k) % 4) * 128, 128), :],
                        from_p.at[h, k - 1],
                        links.along_p(k),
                    )
                    for k in range(1, 4)
                ]
            )
        )
    own_b = at(2048 + c * 256, 256)
    right[own_b, :] = left[1024:1280, :]
    batch_own = links.start([(right.at[own_b, :], right.at[own_b, :], links.core())])

    def fill(first, height):
        cols = pl.ds(pl.multiple_of(first, 256), 256)
        right_sq[:, cols] = as_row(square_sums(right[cols, :]))
        for i in range(2):
            rows = slice(i * (height // 2), (i + 1) * (height // 2))
            table[rows, cols] = kernel_values(
                left[rows, :], left_sq[rows, :], right[cols, :], right_sq[:, cols]
            )

    theirs = [(1 - c) * 1024 + ((q + k) % 4) * 256 for k in range(4)]
    here = at(c * 256, 256)

    def start_sum_q(h):
        arrived(sum_p[h])
        for i in range(2):
            rows = slice(64 * i, 64 * i + 64)
            sum1[h, rows, :] = (
                part[at(512 * h + p * 128 + 64 * i, 64), :]
                + from_p[h, 0, rows, :]
                + from_p[h, 1, rows, :]
                + from_p[h, 2, rows, :]
            )
        return links.start(
            [
                (
                    sum1.at[h, at(((q + k) % 4) * 32, 32), :],
                    from_q.at[h, k - 1],
                    links.along_q(k),
                )
                for k in range(1, 4)
            ]
        )

    def share(h, owner):
        return sum2.at[h, at((owner // 2) * 8, 8), at((owner % 2) * 128, 128)]

    def start_sum_z(h):
        arrived(sum_q[h])
        sum2[h] = sum1[h, at(q * 32, 32), :] + from_q[h, 0] + from_q[h, 1] + from_q[h, 2]
        return links.start(
            [
                (share(h, (z + k) % 8), from_z.at[h, k - 1], links.along_z(k))
                for k in range(1, 8)
            ]
        )

    def start_resid_z(h):
        arrived(sum_z[h])
        total = share(h, z)[...]
        for k in range(7):
            total = total + from_z[h, k]
        gathered[h, z] = total
        tile = gathered.at[h, z]
        return links.start([(tile, tile, links.along_z(k)) for k in range(1, 8)])

    def resid_rows(h, first, count):
        return resid.at[at(512 * h + first, count), here]

    def start_resid_q(h):
        arrived(resid_z[h])
        rows = [
            jnp.concatenate([gathered[h, 2 * i], gathered[h, 2 * i + 1]], axis=1) for i in range(4)
        ]
        tile = resid_rows(h, p * 128 + q * 32, 32)
        tile[...] = jnp.concatenate(rows, axis=0).astype(BF16)
        return links.start([(tile, tile, links.along_q(k)) for k in range(1, 4)])

    def start_resid_p(h):
        arrived(resid_q[h])
        tile = resid_rows(h, p * 128, 128)
        out = links.start([(tile, tile, links.along_p(k)) for k in range(1, 4)])
        return out, links.start([(tile, tile, links.core())])

    def pass_on(h):
        copies, more = resid_p[h]
        for k, copy in zip((1, 2, 3), copies):
            arrived([copy])
            tile = resid_rows(h, ((p + 4 - k) % 4) * 128, 128)
            more += links.start([(tile, tile, links.core())])
        return more

    fill(blocks[0], 1280)
    arrived(nys_own)
    fill(theirs[0], 1280)
    sum_q = [start_sum_q(0)]
    fill(2048 + c * 256, 1024)
    sum_q.append(start_sum_q(1))
    nys_p += links.start([(piece[1], piece[1], links.along_p(k)) for k in (1, 3)])
    mine = vectors(blocks[0], 256)
    eig_p = links.start([(mine, mine, links.along_p(k)) for k in range(1, 4)])
    arrived(batch_own)
    fill(2304 - c * 256, 1024)
    sum_z = [start_sum_z(0)]
    sum_z.append(start_sum_z(1))
    nys_far = links.start([(nys(blocks[0], 256), nys(blocks[0], 256), links.along_p(2))])
    resid_z = [start_resid_z(0)]
    resid_z.append(start_resid_z(1))
    arrived(nys_p)
    nys_core = links.start(
        [(nys(blocks[k], 256), nys(blocks[k], 256), links.core()) for k in (1, 3)]
    )
    fill(blocks[1], 1280)
    fill(blocks[3], 1280)
    arrived(nys_core)
    fill(theirs[1], 1280)
    fill(theirs[3], 1280)
    resid_q = [start_resid_q(0)]
    resid_q.append(start_resid_q(1))
    arrived(eig_p)
    eig_core = links.start([(vectors(c * 1024, 1024), vectors(c * 1024, 1024), links.core())])
    arrived(nys_far)
    nys_last = links.start([(nys(blocks[2], 256), nys(blocks[2], 256), links.core())])
    fill(blocks[2], 1280)
    resid_p = [start_resid_p(0)]
    resid_p.append(start_resid_p(1))
    arrived(eig_core)

    narrow = lax.broadcasted_iota(jnp.int32, (256, 128), 1) < 32

    def split(i, carry):
        rows = at(i * 256, 256)
        some = eig[pl.ds(i * 8, 8), :, :]
        high, middle, low = three(some[:, 0:32, :].reshape(256, 128))
        stack[rows, 0:128] = high
        stack[rows, 128:256] = high
        stack[rows, 256:384] = middle
        stack[rows, 512:640] = low
        rest = some[:, 32:40, :].reshape(64, 128)
        rest = [rest] + [pltpu.roll(rest, 128 - 32 * k, 1) for k in range(1, 4)]
        rest = jnp.concatenate([v.reshape(8, 8, 128) for v in rest], axis=1).reshape(256, 128)
        high, middle, low = three(jnp.where(narrow, rest, 0.0))
        stack[rows, 384:512] = beside(high, high, middle)
        stack[rows, 640:768] = low
        return carry

    lax.fori_loop(0, 8, split, 0)
    arrived(nys_last)
    fill(theirs[2], 1280)

    loads[6].wait()
    wide_corr[...] = jnp.zeros((1, 256), F32)
    wide_corr[:, 0:Q] = small_corr[...]
    product = jnp.dot(table[1024:1280, 0:NYS], stack[...], preferred_element_type=F32)
    value = product[:, 0:128] + product[:, 256:384] + product[:, 512:640]
    high, middle, low = three(value * wide_corr[:, 0:128])
    rows = at(c * 256, 256)
    mixed[rows, 0:128] = high
    mixed[rows, 128:256] = middle
    mixed[rows, 256:384] = low
    value = product[:, 384:512]
    value = value + pltpu.roll(value, 64, 1) + product[:, 640:768]
    high, middle, low = three(jnp.where(narrow, value * wide_corr[:, 128:256], 0.0))
    mixed[rows, 384:512] = beside(high, middle, low)
    mixed_core = links.start([(mixed.at[rows, :], mixed.at[rows, :], links.core())])
    resid_core = pass_on(0) + pass_on(1)
    arrived(mixed_core)
    arrived(resid_core)
    for copy in links.all:
        copy.wait_send()


def tail_kernel(old, stack, table, mixed, resid, out, scaled, coefs, new, sent):
    narrow = lax.broadcasted_iota(jnp.int32, (1024, 128), 1) < 32
    value = jnp.dot(resid[...], mixed[...], preferred_element_type=F32)
    high, middle, _ = three(value[:, 0:128] + value[:, 128:256] + value[:, 256:384])
    scaled[:, 0:128] = high
    scaled[:, 128:256] = middle
    scaled[:, 256:384] = high
    value = value[:, 384:512]
    value = value + pltpu.roll(value, 96, 1) + pltpu.roll(value, 64, 1)
    high, middle, _ = three(jnp.where(narrow, value, 0.0))
    scaled[:, 384:512] = beside(high, middle, high)
    for i in range(4):
        cols = slice(512 * i, 512 * i + 512)
        for k in range(2):
            rows = slice(512 * k, 512 * k + 512)
            coefs[rows, cols] = (-by_rows(scaled[rows, :], stack[cols, 0:512])).astype(BF16)
    coefs[:, NYS : NYS + BATCH] = resid[...]
    copies = []
    for i in range(4):
        cols = slice(256 * i, 256 * i + 256)
        for rows in (slice(0, 512), slice(512, OUT)):
            change = by_rows(coefs[rows.start : rows.start + 512, :], table[cols, :])
            new[rows, cols] = old[rows, cols] - (RATE / BATCH) * change[0 : rows.stop - rows.start]
        copies.append(pltpu.make_async_copy(new.at[:, cols], out.at[:, cols], sent.at[i]))
        copies[-1].start()
    for copy in copies:
        copy.wait()


def by_rows(a, b):
    return lax.dot_general(a, b, (((1,), (1,)), ((), ())), preferred_element_type=F32)


def beside(a, b, c):
    a, b, c = (v.astype(F32) for v in (a, b, c))
    return (a + pltpu.roll(b, 32, 1) + pltpu.roll(c, 64, 1)).astype(BF16)


def per_device(centers, weights, batch_points, labels, nystrom_points, eigvecs, corrections):
    hbm = pl.BlockSpec(memory_space=pltpu.HBM)
    vmem = pltpu.VMEM
    inner = pl.BlockSpec(memory_space=vmem)
    handed = pl.pallas_call(
        step_kernel,
        out_shape=(
            jax.ShapeDtypeStruct((NYS, 768), BF16),
            jax.ShapeDtypeStruct((1280, NYS + BATCH), BF16),
            jax.ShapeDtypeStruct((BATCH, 512), BF16),
            jax.ShapeDtypeStruct((1024, BATCH), BF16),
        ),
        in_specs=[hbm] * 7,
        out_specs=(inner,) * 4,
        scratch_shapes=[
            vmem((2304, FEATURES), BF16),
            vmem((1280, 1), F32),
            vmem((2560, FEATURES), BF16),
            vmem((1, 2560), F32),
            vmem((1, 2048), F32),
            vmem((2, FEATURES), BF16),
            vmem((2, OUT), F32),
            vmem((64, Q), F32),
            vmem((1, Q), F32),
            vmem((1, 256), F32),
            vmem((256, FEATURES), BF16),
            vmem((8, 256, 128), F32),
            vmem((8, 256, 128), F32),
            vmem((OUT, CEN), F32),
            vmem((1024, 2048), BF16),
            vmem((64, 40, 128), F32),
            vmem((256, 2048), BF16),
            vmem((1024, 256), F32),
            vmem((1024, 256), F32),
            vmem((2, 128, 256), F32),
            vmem((2, 32, 256), F32),
            vmem((2, 3, 128, 256), F32),
            vmem((2, 3, 32, 256), F32),
            vmem((2, 7, 8, 128), F32),
            vmem((2, 8, 8, 128), F32),
            pltpu.SemaphoreType.DMA((110,)),
            pltpu.SemaphoreType.DMA((110,)),
            pltpu.SemaphoreType.DMA((7,)),
        ],
        compiler_params=pltpu.CompilerParams(
            collective_id=0, has_side_effects=True, vmem_limit_bytes=38 << 20
        ),
        name="step",
    )(
        *(
            pltpu.with_memory_space_constraint(v, pltpu.HBM)
            for v in (
                centers,
                weights.T,
                batch_points,
                labels,
                nystrom_points,
                eigvecs,
                corrections.reshape(1, Q),
            )
        )
    )
    return pl.pallas_call(
        tail_kernel,
        out_shape=jax.ShapeDtypeStruct((OUT, CEN), F32),
        in_specs=[inner] * 5,
        out_specs=hbm,
        scratch_shapes=[
            vmem((1024, 512), BF16),
            vmem((1024, NYS + BATCH), BF16),
            vmem((OUT, CEN), F32),
            pltpu.SemaphoreType.DMA((4,)),
        ],
        compiler_params=pltpu.CompilerParams(vmem_limit_bytes=24 << 20),
        name="tail",
    )(weights.T, *handed).T


def solution(mesh):
    every = P(("narrow", "wide", "nys"), None)
    some = P(("narrow", "nys"), None)
    return jax.shard_map(
        per_device,
        mesh=mesh,
        in_specs=(every, every, every, every, some, some, P()),
        out_specs=every,
        check_vma=False,
    )
```

```python
import math

import jax
import jax.numpy as jnp
from jax import lax
from jax.experimental import pallas as pl
from jax.experimental.pallas import tpu as pltpu
from jax.sharding import PartitionSpec as P

RATE = 16.0
SPREAD = 4.0
MESH = pl.DeviceIdType.MESH
F32, BF16 = jnp.float32, jnp.bfloat16

FEATURES = 1024
CEN = 1024
OUT = 1000
NYS = 2048
BATCH = 512
Q = 160
UNIT = (math.log2(math.e) / SPREAD) ** 2
TOP = math.sqrt(2.0 * FEATURES) * math.log2(math.e) / SPREAD


def device(x, y, z, c):
    return (y * 2 + z % 2, (z // 2) * 2 + c, x)


class Links:
    def __init__(self, send, recv):
        n, w, self.x = (lax.axis_index(a) for a in ("narrow", "wide", "nys"))
        self.y, self.c = n // 2, w % 2
        self.z = (w // 2) * 2 + n % 2
        self.p = self.x * (1 - self.c) + self.y * self.c
        self.q = self.y * (1 - self.c) + self.x * self.c
        self.send, self.recv, self.next, self.all = send, recv, 0, []

    def core(self):
        return device(self.x, self.y, self.z, 1 - self.c)

    def along_p(self, k):
        c = self.c
        return device((self.x + k * (1 - c)) % 4, (self.y + k * c) % 4, self.z, c)

    def along_q(self, k):
        c = self.c
        return device((self.x + k * c) % 4, (self.y + k * (1 - c)) % 4, self.z, c)

    def along_z(self, k):
        return device(self.x, self.y, (self.z + k) % 8, self.c)

    def z_pair(self):
        return device(self.x, self.y, self.z + 1 - 2 * (self.z % 2), self.c)

    def peers(self):
        out = [self.core()]
        out += [self.along_p(k) for k in range(1, 4)]
        out += [self.along_q(k) for k in range(1, 4)]
        out += [self.along_z(k) for k in range(1, 8)]
        return out

    def start(self, pairs):
        out = []
        for src, dst, peer in pairs:
            copy = pltpu.make_async_remote_copy(
                src_ref=src,
                dst_ref=dst,
                send_sem=self.send.at[self.next],
                recv_sem=self.recv.at[self.next],
                device_id=peer,
                device_id_type=MESH,
            )
            self.next += 1
            copy.start()
            out.append(copy)
        self.all += out
        return out


def arrived(copies):
    for copy in copies:
        copy.wait_recv()


def at(start, size, unit=None):
    if isinstance(start, int):
        return slice(start, start + size)
    return pl.ds(pl.multiple_of(start, unit or size), size)


def square_sums(points):
    wide = points.astype(F32)
    return jnp.sum(wide * wide, axis=1, keepdims=True) * UNIT


def as_row(column):
    return jnp.transpose(jnp.broadcast_to(column, (column.shape[0], 128)))[0:1, :]


def kernel_values(left, left_sq, right, right_sq):
    cross = lax.dot_general(left, right, (((1,), (1,)), ((), ())), preferred_element_type=F32)
    dist_sq = jnp.maximum((left_sq + right_sq) - (2.0 * UNIT) * cross, 1e-30)
    return jnp.exp2(TOP - dist_sq * lax.rsqrt(dist_sq)).astype(BF16)


def three(value):
    high = value.astype(BF16)
    rest = value - high.astype(F32)
    middle = rest.astype(BF16)
    low = (rest - middle.astype(F32)).astype(BF16)
    return high, middle, low


def step_kernel(
    centers,
    weights,
    batch,
    labels,
    nystrom,
    eigvecs,
    corrections,
    stack,
    table,
    mixed,
    resid,
    coefs,
    left,
    left_sq,
    right,
    right_sq,
    center_sq,
    small_batch,
    small_labels,
    small_eig,
    small_corr,
    wide_corr,
    tiles,
    wide_tiles,
    wide_batch,
    old,
    rounded,
    eig,
    k_batch,
    part,
    placed,
    sum1,
    sum2,
    from_p,
    from_q,
    from_z,
    gathered,
    scaled,
    send,
    recv,
    local,
):
    links = Links(send, recv)
    c, p, q, z = links.c, links.p, links.q, links.z
    group = p * 4 + q

    own_n = c * 1024 + p * 256 + q * 64 + (z % 2) * 32
    loads = [
        (batch, small_batch),
        (labels, small_labels),
        (eigvecs, small_eig),
        (nystrom.at[at(c * 32, 32), :], right.at[at(own_n, 32), :]),
        (centers, left.at[0:1024, :]),
        (weights, old),
        (corrections, small_corr),
    ]
    loads = [pltpu.make_async_copy(s, d, local.at[i]) for i, (s, d) in enumerate(loads)]
    for load in loads:
        load.start()
    barrier = pltpu.get_barrier_semaphore()
    peers = links.peers()
    for peer in peers:
        pl.semaphore_signal(barrier, inc=1, device_id=peer, device_id_type=MESH)

    loads[0].wait()
    pair = small_batch[...].astype(F32)
    for r in range(2):
        for j in range(8):
            wide_tiles[0, 8 * r + j : 8 * r + j + 1, :] = pair[r : r + 1, 128 * j : 128 * j + 128]
    tiles[at(group * 16, 16), at(z * 128, 128)] = wide_tiles[0, 0:16, :].astype(BF16)
    loads[2].wait()
    own_e = own_n // 32
    mine = small_eig[at(c * 32, 32), :]
    eig[own_e, 0:32, :] = mine[:, 0:128]
    for k in range(4):
        eig[own_e, 32:40, 32 * k : 32 * k + 32] = mine[8 * k : 8 * k + 8, 128:Q]
    loads[3].wait()
    pl.semaphore_wait(barrier, len(peers))

    def nys(first, count):
        return right.at[at(first, count, count), :]

    def vectors(first, count):
        return eig.at[pl.ds(first // 32, count // 32)]

    tile = tiles.at[at(group * 16, 16), at(z * 128, 128)]
    batch_q = links.start([(tile, tile, links.along_q(k)) for k in range(1, 4)])
    own = [nys(own_n, 32), vectors(own_n, 32)]
    nys_z = links.start([(o, o, links.z_pair()) for o in own])
    loads[4].wait()
    swap = links.start([(left.at[0:1024, :], left.at[1280:2304, :], links.core())])

    arrived(batch_q)
    tile = tiles.at[at(p * 64, 64), at(z * 128, 128)]
    batch_z = links.start([(tile, tile, links.along_z(k)) for k in range(1, 8)])
    arrived(nys_z)
    own_q = c * 1024 + p * 256 + q * 64
    own = [nys(own_q, 64), vectors(own_q, 64)]
    nys_q = links.start([(o, o, links.along_q(k)) for k in range(1, 4) for o in own])

    loads[5].wait()
    for i in range(7):
        rows = slice(128 * i, 128 * i + 128)
        rounded[rows, 0:1024] = old[rows, :].astype(BF16)
    last = jnp.concatenate([old[896:OUT, :], jnp.zeros((1024 - OUT, CEN), F32)], axis=0)
    rounded[896:1024, 0:1024] = last.astype(BF16)
    swap += links.start([(rounded.at[:, 0:1024], rounded.at[:, 1024:2048], links.core())])

    arrived(batch_z)
    block = tiles.at[at(p * 64, 64), :]
    batch_p = links.start([(block, block, links.along_p(k)) for k in range(1, 4)])

    def own_squares(i, carry):
        rows = at(i * 256, 256)
        value = square_sums(left[rows, :])
        left_sq[rows, :] = value
        center_sq[:, rows] = as_row(value)
        return carry

    lax.fori_loop(0, 4, own_squares, 0)
    loads[1].wait()
    wide_labels = [
        jnp.transpose(jnp.broadcast_to(small_labels[r : r + 1, :], (128, OUT))) for r in range(2)
    ]
    lane = lax.broadcasted_iota(jnp.int32, (OUT, 128), 1)
    for i in range(2):
        point = group * 16 + z - 128 * i
        placed[0:OUT, 128 * i : 128 * i + 128] = jnp.where(
            lane == point, wide_labels[0], jnp.where(lane == point + 8, wide_labels[1], 0.0)
        )
    placed[OUT:1024, :] = jnp.zeros((1024 - OUT, 256), F32)
    arrived(nys_q)
    blocks = [c * 1024 + ((p + k) % 4) * 256 for k in range(4)]
    nys_own = links.start([(nys(blocks[0], 256), nys(blocks[0], 256), links.core())])
    arrived(swap)

    def other_squares(i, carry):
        rows = pl.ds(pl.multiple_of(1280 + i * 256, 256), 256)
        center_sq[:, pl.ds(pl.multiple_of(1024 + i * 256, 256), 256)] = as_row(
            square_sums(left[rows, :])
        )
        return carry

    lax.fori_loop(0, 4, other_squares, 0)
    arrived(batch_p)
    piece = [nys(blocks[0] + 128 * i, 128) for i in range(2)]
    nys_p = links.start([(piece[0], piece[0], links.along_p(k)) for k in (1, 3)])

    for zz in range(8):
        wide_tiles[zz] = tiles[:, 128 * zz : 128 * zz + 128].astype(F32)
    for zz in range(8):
        for j in range(8):
            wide_batch[j, pl.ds(zz, 32, stride=8), :] = wide_tiles[zz, pl.ds(j, 32, stride=8), :]
    squares = jnp.zeros((256, 128), F32)
    for j in range(8):
        wide = wide_batch[j]
        left[1024:1280, 128 * j : 128 * j + 128] = wide.astype(BF16)
        squares = squares + wide * wide
    left_sq[1024:1280, :] = jnp.sum(squares, axis=1, keepdims=True) * UNIT
    points, points_sq = left[1024:1280, :], left_sq[1024:1280, :]
    for i in range(8):
        first = i * 256 if i < 4 else 256 + i * 256
        k_batch[:, 256 * i : 256 * i + 256] = kernel_values(
            points, points_sq, left[first : first + 256, :], center_sq[:, 256 * i : 256 * i + 256]
        )
    scale = (CEN * 256) ** (-0.5)
    sum_p = []
    for h in range(2):
        for i in range(2):
            rows = slice(512 * h + 256 * i, 512 * h + 256 * i + 256)
            part[rows, :] = scale * by_rows(rounded[rows, :], k_batch[...]) - placed[rows, :]
        sum_p.append(
            links.start(
                [
                    (
                        part.at[at(512 * h + ((p + k) % 4) * 128, 128), :],
                        from_p.at[h, k - 1],
                        links.along_p(k),
                    )
                    for k in range(1, 4)
                ]
            )
        )
    own_b = at(2048 + c * 256, 256)
    right[own_b, :] = left[1024:1280, :]
    batch_own = links.start([(right.at[own_b, :], right.at[own_b, :], links.core())])

    def fill(first, height):
        cols = pl.ds(pl.multiple_of(first, 256), 256)
        right_sq[:, cols] = as_row(square_sums(right[cols, :]))
        for i in range(2):
            rows = slice(i * (height // 2), (i + 1) * (height // 2))
            table[rows, cols] = kernel_values(
                left[rows, :], left_sq[rows, :], right[cols, :], right_sq[:, cols]
            )

    theirs = [(1 - c) * 1024 + ((q + k) % 4) * 256 for k in range(4)]
    here = at(c * 256, 256)

    def start_sum_q(h):
        arrived(sum_p[h])
        for i in range(2):
            rows = slice(64 * i, 64 * i + 64)
            sum1[h, rows, :] = (
                part[at(512 * h + p * 128 + 64 * i, 64), :]
                + from_p[h, 0, rows, :]
                + from_p[h, 1, rows, :]
                + from_p[h, 2, rows, :]
            )
        return links.start(
            [
                (
                    sum1.at[h, at(((q + k) % 4) * 32, 32), :],
                    from_q.at[h, k - 1],
                    links.along_q(k),
                )
                for k in range(1, 4)
            ]
        )

    def share(h, owner):
        return sum2.at[h, at((owner // 2) * 8, 8), at((owner % 2) * 128, 128)]

    def start_sum_z(h):
        arrived(sum_q[h])
        sum2[h] = sum1[h, at(q * 32, 32), :] + from_q[h, 0] + from_q[h, 1] + from_q[h, 2]
        return links.start(
            [
                (share(h, (z + k) % 8), from_z.at[h, k - 1], links.along_z(k))
                for k in range(1, 8)
            ]
        )

    def start_resid_z(h):
        arrived(sum_z[h])
        total = share(h, z)[...]
        for k in range(7):
            total = total + from_z[h, k]
        gathered[h, z] = total
        tile = gathered.at[h, z]
        return links.start([(tile, tile, links.along_z(k)) for k in range(1, 8)])

    def resid_rows(h, first, count):
        return resid.at[at(512 * h + first, count), here]

    def start_resid_q(h):
        arrived(resid_z[h])
        rows = [
            jnp.concatenate([gathered[h, 2 * i], gathered[h, 2 * i + 1]], axis=1) for i in range(4)
        ]
        tile = resid_rows(h, p * 128 + q * 32, 32)
        tile[...] = jnp.concatenate(rows, axis=0).astype(BF16)
        return links.start([(tile, tile, links.along_q(k)) for k in range(1, 4)])

    def start_resid_p(h):
        arrived(resid_q[h])
        tile = resid_rows(h, p * 128, 128)
        out = links.start([(tile, tile, links.along_p(k)) for k in range(1, 4)])
        return out, links.start([(tile, tile, links.core())])

    def pass_on(h):
        copies, more = resid_p[h]
        for k, copy in zip((1, 2, 3), copies):
            arrived([copy])
            tile = resid_rows(h, ((p + 4 - k) % 4) * 128, 128)
            more += links.start([(tile, tile, links.core())])
        return more

    fill(blocks[0], 1280)
    arrived(nys_own)
    fill(theirs[0], 1280)
    sum_q = [start_sum_q(0)]
    fill(2048 + c * 256, 1024)
    sum_q.append(start_sum_q(1))
    nys_p += links.start([(piece[1], piece[1], links.along_p(k)) for k in (1, 3)])
    mine = vectors(blocks[0], 256)
    eig_p = links.start([(mine, mine, links.along_p(k)) for k in range(1, 4)])
    arrived(batch_own)
    fill(2304 - c * 256, 1024)
    sum_z = [start_sum_z(0)]
    sum_z.append(start_sum_z(1))
    nys_far = links.start([(nys(blocks[0], 256), nys(blocks[0], 256), links.along_p(2))])
    resid_z = [start_resid_z(0)]
    resid_z.append(start_resid_z(1))
    arrived(nys_p)
    nys_core = links.start(
        [(nys(blocks[k], 256), nys(blocks[k], 256), links.core()) for k in (1, 3)]
    )
    fill(blocks[1], 1280)
    fill(blocks[3], 1280)
    arrived(nys_core)
    fill(theirs[1], 1280)
    fill(theirs[3], 1280)
    resid_q = [start_resid_q(0)]
    resid_q.append(start_resid_q(1))
    arrived(eig_p)
    eig_core = links.start([(vectors(c * 1024, 1024), vectors(c * 1024, 1024), links.core())])
    arrived(nys_far)
    nys_last = links.start([(nys(blocks[2], 256), nys(blocks[2], 256), links.core())])
    fill(blocks[2], 1280)
    resid_p = [start_resid_p(0)]
    resid_p.append(start_resid_p(1))
    arrived(eig_core)

    narrow = lax.broadcasted_iota(jnp.int32, (256, 128), 1) < 32

    def split(i, carry):
        rows = at(i * 256, 256)
        some = eig[pl.ds(i * 8, 8), :, :]
        high, middle, low = three(some[:, 0:32, :].reshape(256, 128))
        stack[rows, 0:128] = high
        stack[rows, 128:256] = high
        stack[rows, 256:384] = middle
        stack[rows, 512:640] = low
        rest = some[:, 32:40, :].reshape(64, 128)
        rest = [rest] + [pltpu.roll(rest, 128 - 32 * k, 1) for k in range(1, 4)]
        rest = jnp.concatenate([v.reshape(8, 8, 128) for v in rest], axis=1).reshape(256, 128)
        high, middle, low = three(jnp.where(narrow, rest, 0.0))
        stack[rows, 384:512] = beside(high, high, middle)
        stack[rows, 640:768] = low
        return carry

    lax.fori_loop(0, 8, split, 0)
    arrived(nys_last)
    fill(theirs[2], 1280)

    loads[6].wait()
    wide_corr[...] = jnp.zeros((1, 256), F32)
    wide_corr[:, 0:Q] = small_corr[...]
    product = jnp.dot(table[1024:1280, 0:NYS], stack[...], preferred_element_type=F32)
    value = product[:, 0:128] + product[:, 256:384] + product[:, 512:640]
    high, middle, low = three(value * wide_corr[:, 0:128])
    rows = at(c * 256, 256)
    mixed[rows, 0:128] = high
    mixed[rows, 128:256] = middle
    mixed[rows, 256:384] = low
    value = product[:, 384:512]
    value = value + pltpu.roll(value, 64, 1) + product[:, 640:768]
    high, middle, low = three(jnp.where(narrow, value * wide_corr[:, 128:256], 0.0))
    mixed[rows, 384:512] = beside(high, middle, low)
    mixed_core = links.start([(mixed.at[rows, :], mixed.at[rows, :], links.core())])
    resid_core = pass_on(0)
    arrived(mixed_core)
    arrived(resid_core)
    project(resid[0:512, :], mixed, scaled)
    resid_core = pass_on(1)
    correct(scaled, stack, coefs)
    arrived(resid_core)
    for copy in links.all:
        copy.wait_send()


def project(resid, mixed, scaled):
    narrow = lax.broadcasted_iota(jnp.int32, (512, 128), 1) < 32
    value = jnp.dot(resid, mixed[...], preferred_element_type=F32)
    high, middle, _ = three(value[:, 0:128] + value[:, 128:256] + value[:, 256:384])
    scaled[:, 0:128] = high
    scaled[:, 128:256] = middle
    scaled[:, 256:384] = high
    value = value[:, 384:512]
    value = value + pltpu.roll(value, 96, 1) + pltpu.roll(value, 64, 1)
    high, middle, _ = three(jnp.where(narrow, value, 0.0))
    scaled[:, 384:512] = beside(high, middle, high)


def correct(scaled, stack, coefs):
    for i in range(4):
        cols = slice(512 * i, 512 * i + 512)
        coefs[:, cols] = (-by_rows(scaled[...], stack[cols, 0:512])).astype(BF16)


def tail_kernel(old, stack, table, mixed, resid, first, out, scaled, coefs, new, sent):
    coefs[0:512, 0:NYS] = first[...]
    project(resid[512:1024, :], mixed, scaled)
    correct(scaled, stack, coefs.at[512:1024, :])
    coefs[:, NYS : NYS + BATCH] = resid[...]
    copies = []
    for i in range(4):
        cols = slice(256 * i, 256 * i + 256)
        for rows in (slice(0, 512), slice(512, OUT)):
            change = by_rows(coefs[rows.start : rows.start + 512, :], table[cols, :])
            new[rows, cols] = old[rows, cols] - (RATE / BATCH) * change[0 : rows.stop - rows.start]
        copies.append(pltpu.make_async_copy(new.at[:, cols], out.at[:, cols], sent.at[i]))
        copies[-1].start()
    for copy in copies:
        copy.wait()


def by_rows(a, b):
    return lax.dot_general(a, b, (((1,), (1,)), ((), ())), preferred_element_type=F32)


def beside(a, b, c):
    a, b, c = (v.astype(F32) for v in (a, b, c))
    return (a + pltpu.roll(b, 32, 1) + pltpu.roll(c, 64, 1)).astype(BF16)


def per_device(centers, weights, batch_points, labels, nystrom_points, eigvecs, corrections):
    hbm = pl.BlockSpec(memory_space=pltpu.HBM)
    vmem = pltpu.VMEM
    inner = pl.BlockSpec(memory_space=vmem)
    handed = pl.pallas_call(
        step_kernel,
        out_shape=(
            jax.ShapeDtypeStruct((NYS, 768), BF16),
            jax.ShapeDtypeStruct((1280, NYS + BATCH), BF16),
            jax.ShapeDtypeStruct((BATCH, 512), BF16),
            jax.ShapeDtypeStruct((1024, BATCH), BF16),
            jax.ShapeDtypeStruct((512, NYS), BF16),
        ),
        in_specs=[hbm] * 7,
        out_specs=(inner,) * 5,
        scratch_shapes=[
            vmem((2304, FEATURES), BF16),
            vmem((1280, 1), F32),
            vmem((2560, FEATURES), BF16),
            vmem((1, 2560), F32),
            vmem((1, 2048), F32),
            vmem((2, FEATURES), BF16),
            vmem((2, OUT), F32),
            vmem((64, Q), F32),
            vmem((1, Q), F32),
            vmem((1, 256), F32),
            vmem((256, FEATURES), BF16),
            vmem((8, 256, 128), F32),
            vmem((8, 256, 128), F32),
            vmem((OUT, CEN), F32),
            vmem((1024, 2048), BF16),
            vmem((64, 40, 128), F32),
            vmem((256, 2048), BF16),
            vmem((1024, 256), F32),
            vmem((1024, 256), F32),
            vmem((2, 128, 256), F32),
            vmem((2, 32, 256), F32),
            vmem((2, 3, 128, 256), F32),
            vmem((2, 3, 32, 256), F32),
            vmem((2, 7, 8, 128), F32),
            vmem((2, 8, 8, 128), F32),
            vmem((512, 512), BF16),
            pltpu.SemaphoreType.DMA((110,)),
            pltpu.SemaphoreType.DMA((110,)),
            pltpu.SemaphoreType.DMA((7,)),
        ],
        compiler_params=pltpu.CompilerParams(
            collective_id=0, has_side_effects=True, vmem_limit_bytes=38 << 20
        ),
        name="step",
    )(
        *(
            pltpu.with_memory_space_constraint(v, pltpu.HBM)
            for v in (
                centers,
                weights.T,
                batch_points,
                labels,
                nystrom_points,
                eigvecs,
                corrections.reshape(1, Q),
            )
        )
    )
    return pl.pallas_call(
        tail_kernel,
        out_shape=jax.ShapeDtypeStruct((OUT, CEN), F32),
        in_specs=[inner] * 6,
        out_specs=hbm,
        scratch_shapes=[
            vmem((512, 512), BF16),
            vmem((1024, NYS + BATCH), BF16),
            vmem((OUT, CEN), F32),
            pltpu.SemaphoreType.DMA((4,)),
        ],
        compiler_params=pltpu.CompilerParams(vmem_limit_bytes=24 << 20),
        name="tail",
    )(weights.T, *handed).T


def solution(mesh):
    every = P(("narrow", "wide", "nys"), None)
    some = P(("narrow", "nys"), None)
    return jax.shard_map(
        per_device,
        mesh=mesh,
        in_specs=(every, every, every, every, some, some, P()),
        out_specs=every,
        check_vma=False,
    )
```

```python
import math

import jax
import jax.numpy as jnp
from jax import lax
from jax.experimental import pallas as pl
from jax.experimental.pallas import tpu as pltpu
from jax.sharding import PartitionSpec as P

RATE = 16.0
SPREAD = 4.0
MESH = pl.DeviceIdType.MESH
F32, BF16 = jnp.float32, jnp.bfloat16

FEATURES = 1024
CEN = 1024
OUT = 1000
NYS = 2048
BATCH = 512
Q = 160
UNIT = (math.log2(math.e) / SPREAD) ** 2
TOP = math.sqrt(2.0 * FEATURES) * math.log2(math.e) / SPREAD


def device(x, y, z, c):
    return (y * 2 + z % 2, (z // 2) * 2 + c, x)


class Links:
    def __init__(self, send, recv):
        n, w, self.x = (lax.axis_index(a) for a in ("narrow", "wide", "nys"))
        self.y, self.c = n // 2, w % 2
        self.z = (w // 2) * 2 + n % 2
        self.p = self.x * (1 - self.c) + self.y * self.c
        self.q = self.y * (1 - self.c) + self.x * self.c
        self.send, self.recv, self.next, self.all = send, recv, 0, []

    def core(self):
        return device(self.x, self.y, self.z, 1 - self.c)

    def along_p(self, k):
        c = self.c
        return device((self.x + k * (1 - c)) % 4, (self.y + k * c) % 4, self.z, c)

    def along_q(self, k):
        c = self.c
        return device((self.x + k * c) % 4, (self.y + k * (1 - c)) % 4, self.z, c)

    def along_z(self, k):
        return device(self.x, self.y, (self.z + k) % 8, self.c)

    def z_pair(self):
        return device(self.x, self.y, self.z + 1 - 2 * (self.z % 2), self.c)

    def peers(self):
        out = [self.core()]
        out += [self.along_p(k) for k in range(1, 4)]
        out += [self.along_q(k) for k in range(1, 4)]
        out += [self.along_z(k) for k in range(1, 8)]
        return out

    def start(self, pairs):
        out = []
        for src, dst, peer in pairs:
            copy = pltpu.make_async_remote_copy(
                src_ref=src,
                dst_ref=dst,
                send_sem=self.send.at[self.next],
                recv_sem=self.recv.at[self.next],
                device_id=peer,
                device_id_type=MESH,
            )
            self.next += 1
            copy.start()
            out.append(copy)
        self.all += out
        return out


def arrived(copies):
    for copy in copies:
        copy.wait_recv()


def at(start, size, unit=None):
    if isinstance(start, int):
        return slice(start, start + size)
    return pl.ds(pl.multiple_of(start, unit or size), size)


def square_sums(points):
    wide = points.astype(F32)
    return jnp.sum(wide * wide, axis=1, keepdims=True) * UNIT


def as_row(column):
    return jnp.transpose(jnp.broadcast_to(column, (column.shape[0], 128)))[0:1, :]


def kernel_values(left, left_sq, right, right_sq):
    cross = lax.dot_general(left, right, (((1,), (1,)), ((), ())), preferred_element_type=F32)
    dist_sq = jnp.maximum((left_sq + right_sq) - (2.0 * UNIT) * cross, 1e-30)
    return jnp.exp2(TOP - dist_sq * lax.rsqrt(dist_sq)).astype(BF16)


def three(value):
    high = value.astype(BF16)
    rest = value - high.astype(F32)
    middle = rest.astype(BF16)
    low = (rest - middle.astype(F32)).astype(BF16)
    return high, middle, low


def step_kernel(
    centers,
    weights,
    batch,
    labels,
    nystrom,
    eigvecs,
    corrections,
    stack,
    table,
    mixed,
    resid,
    coefs,
    left,
    left_sq,
    right,
    right_sq,
    center_sq,
    small_batch,
    small_labels,
    small_eig,
    small_corr,
    wide_corr,
    tiles,
    wide_tiles,
    wide_batch,
    old,
    rounded,
    eig,
    k_batch,
    part,
    placed,
    sum1,
    sum2,
    from_p,
    from_q,
    from_z,
    gathered,
    scaled,
    send,
    recv,
    local,
):
    links = Links(send, recv)
    c, p, q, z = links.c, links.p, links.q, links.z
    group = p * 4 + q

    own_n = c * 1024 + p * 256 + q * 64 + (z % 2) * 32
    loads = [
        (batch, small_batch),
        (labels, small_labels),
        (eigvecs, small_eig),
        (nystrom.at[at(c * 32, 32), :], right.at[at(own_n, 32), :]),
        (centers, left.at[0:1024, :]),
        (weights, old),
        (corrections, small_corr),
    ]
    loads = [pltpu.make_async_copy(s, d, local.at[i]) for i, (s, d) in enumerate(loads)]
    for load in loads:
        load.start()
    barrier = pltpu.get_barrier_semaphore()
    peers = links.peers()
    for peer in peers:
        pl.semaphore_signal(barrier, inc=1, device_id=peer, device_id_type=MESH)

    loads[0].wait()
    pair = small_batch[...].astype(F32)
    for r in range(2):
        for j in range(8):
            wide_tiles[0, 8 * r + j : 8 * r + j + 1, :] = pair[r : r + 1, 128 * j : 128 * j + 128]
    tiles[at(group * 16, 16), at(z * 128, 128)] = wide_tiles[0, 0:16, :].astype(BF16)
    loads[2].wait()
    own_e = own_n // 32
    mine = small_eig[at(c * 32, 32), :]
    eig[own_e, 0:32, :] = mine[:, 0:128]
    for k in range(4):
        eig[own_e, 32:40, 32 * k : 32 * k + 32] = mine[8 * k : 8 * k + 8, 128:Q]
    loads[3].wait()
    pl.semaphore_wait(barrier, len(peers))

    def nys(first, count):
        return right.at[at(first, count, count), :]

    def vectors(first, count):
        return eig.at[pl.ds(first // 32, count // 32)]

    tile = tiles.at[at(group * 16, 16), at(z * 128, 128)]
    batch_q = links.start([(tile, tile, links.along_q(k)) for k in range(1, 4)])
    own = [nys(own_n, 32), vectors(own_n, 32)]
    nys_z = links.start([(o, o, links.z_pair()) for o in own])
    loads[4].wait()
    swap = links.start([(left.at[0:1024, :], left.at[1280:2304, :], links.core())])

    arrived(batch_q)
    tile = tiles.at[at(p * 64, 64), at(z * 128, 128)]
    batch_z = links.start([(tile, tile, links.along_z(k)) for k in range(1, 8)])
    arrived(nys_z)
    own_q = c * 1024 + p * 256 + q * 64
    own = [nys(own_q, 64), vectors(own_q, 64)]
    nys_q = links.start([(o, o, links.along_q(k)) for k in range(1, 4) for o in own])

    loads[5].wait()
    for i in range(7):
        rows = slice(128 * i, 128 * i + 128)
        rounded[rows, 0:1024] = old[rows, :].astype(BF16)
    last = jnp.concatenate([old[896:OUT, :], jnp.zeros((1024 - OUT, CEN), F32)], axis=0)
    rounded[896:1024, 0:1024] = last.astype(BF16)
    swap += links.start([(rounded.at[:, 0:1024], rounded.at[:, 1024:2048], links.core())])

    arrived(batch_z)
    block = tiles.at[at(p * 64, 64), :]
    batch_p = links.start([(block, block, links.along_p(k)) for k in range(1, 4)])

    def own_squares(i, carry):
        rows = at(i * 256, 256)
        value = square_sums(left[rows, :])
        left_sq[rows, :] = value
        center_sq[:, rows] = as_row(value)
        return carry

    lax.fori_loop(0, 4, own_squares, 0)
    loads[1].wait()
    wide_labels = [
        jnp.transpose(jnp.broadcast_to(small_labels[r : r + 1, :], (128, OUT))) for r in range(2)
    ]
    lane = lax.broadcasted_iota(jnp.int32, (OUT, 128), 1)
    for i in range(2):
        point = group * 16 + z - 128 * i
        placed[0:OUT, 128 * i : 128 * i + 128] = jnp.where(
            lane == point, wide_labels[0], jnp.where(lane == point + 8, wide_labels[1], 0.0)
        )
    placed[OUT:1024, :] = jnp.zeros((1024 - OUT, 256), F32)
    arrived(nys_q)
    blocks = [c * 1024 + ((p + k) % 4) * 256 for k in range(4)]
    nys_own = links.start([(nys(blocks[0], 256), nys(blocks[0], 256), links.core())])
    arrived(swap)

    def other_squares(i, carry):
        rows = pl.ds(pl.multiple_of(1280 + i * 256, 256), 256)
        center_sq[:, pl.ds(pl.multiple_of(1024 + i * 256, 256), 256)] = as_row(
            square_sums(left[rows, :])
        )
        return carry

    lax.fori_loop(0, 4, other_squares, 0)
    arrived(batch_p)
    piece = [nys(blocks[0] + 128 * i, 128) for i in range(2)]
    nys_p = links.start([(piece[0], piece[0], links.along_p(k)) for k in (1, 3)])

    for zz in range(8):
        wide_tiles[zz] = tiles[:, 128 * zz : 128 * zz + 128].astype(F32)
    for zz in range(8):
        for j in range(8):
            wide_batch[j, pl.ds(zz, 32, stride=8), :] = wide_tiles[zz, pl.ds(j, 32, stride=8), :]
    squares = jnp.zeros((256, 128), F32)
    for j in range(8):
        wide = wide_batch[j]
        left[1024:1280, 128 * j : 128 * j + 128] = wide.astype(BF16)
        squares = squares + wide * wide
    left_sq[1024:1280, :] = jnp.sum(squares, axis=1, keepdims=True) * UNIT
    points, points_sq = left[1024:1280, :], left_sq[1024:1280, :]
    for i in range(8):
        first = i * 256 if i < 4 else 256 + i * 256
        k_batch[:, 256 * i : 256 * i + 256] = kernel_values(
            points, points_sq, left[first : first + 256, :], center_sq[:, 256 * i : 256 * i + 256]
        )
    scale = (CEN * 256) ** (-0.5)
    sum_p = []
    for h in range(2):
        for i in range(2):
            rows = slice(512 * h + 256 * i, 512 * h + 256 * i + 256)
            part[rows, :] = scale * by_rows(rounded[rows, :], k_batch[...]) - placed[rows, :]
        sum_p.append(
            links.start(
                [
                    (
                        part.at[at(512 * h + ((p + k) % 4) * 128, 128), :],
                        from_p.at[h, k - 1],
                        links.along_p(k),
                    )
                    for k in range(1, 4)
                ]
            )
        )
    own_b = at(2048 + c * 256, 256)
    right[own_b, :] = left[1024:1280, :]
    batch_own = links.start([(right.at[own_b, :], right.at[own_b, :], links.core())])

    def fill(first, end, begin=0, norms=True):
        cols = pl.ds(pl.multiple_of(first, 256), 256)
        if norms:
            right_sq[:, cols] = as_row(square_sums(right[cols, :]))
        count = max((end - begin) // 2, 256)
        for i in range(begin, end, count):
            rows = slice(i, i + count)
            table[rows, cols] = kernel_values(
                left[rows, :], left_sq[rows, :], right[cols, :], right_sq[:, cols]
            )

    theirs = [(1 - c) * 1024 + ((q + k) % 4) * 256 for k in range(4)]
    here = at(c * 256, 256)

    def start_sum_q(h):
        arrived(sum_p[h])
        for i in range(2):
            rows = slice(64 * i, 64 * i + 64)
            sum1[h, rows, :] = (
                part[at(512 * h + p * 128 + 64 * i, 64), :]
                + from_p[h, 0, rows, :]
                + from_p[h, 1, rows, :]
                + from_p[h, 2, rows, :]
            )
        return links.start(
            [
                (
                    sum1.at[h, at(((q + k) % 4) * 32, 32), :],
                    from_q.at[h, k - 1],
                    links.along_q(k),
                )
                for k in range(1, 4)
            ]
        )

    def share(h, owner):
        return sum2.at[h, at((owner // 2) * 8, 8), at((owner % 2) * 128, 128)]

    def start_sum_z(h):
        arrived(sum_q[h])
        sum2[h] = sum1[h, at(q * 32, 32), :] + from_q[h, 0] + from_q[h, 1] + from_q[h, 2]
        return links.start(
            [
                (share(h, (z + k) % 8), from_z.at[h, k - 1], links.along_z(k))
                for k in range(1, 8)
            ]
        )

    def start_resid_z(h):
        arrived(sum_z[h])
        total = share(h, z)[...]
        for k in range(7):
            total = total + from_z[h, k]
        gathered[h, z] = total
        tile = gathered.at[h, z]
        return links.start([(tile, tile, links.along_z(k)) for k in range(1, 8)])

    def resid_rows(h, first, count):
        return resid.at[at(512 * h + first, count), here]

    def start_resid_q(h):
        arrived(resid_z[h])
        rows = [
            jnp.concatenate([gathered[h, 2 * i], gathered[h, 2 * i + 1]], axis=1) for i in range(4)
        ]
        tile = resid_rows(h, p * 128 + q * 32, 32)
        tile[...] = jnp.concatenate(rows, axis=0).astype(BF16)
        return links.start([(tile, tile, links.along_q(k)) for k in range(1, 4)])

    def start_resid_p(h):
        arrived(resid_q[h])
        tile = resid_rows(h, p * 128, 128)
        out = links.start([(tile, tile, links.along_p(k)) for k in range(1, 4)])
        return out, links.start([(tile, tile, links.core())])

    def pass_on(h):
        copies, more = resid_p[h]
        for k, copy in zip((1, 2, 3), copies):
            arrived([copy])
            tile = resid_rows(h, ((p + 4 - k) % 4) * 128, 128)
            more += links.start([(tile, tile, links.core())])
        return more

    fill(blocks[0], 1280)
    arrived(nys_own)
    fill(theirs[0], 1280)
    fill(2048 + c * 256, 1024)
    sum_q = [start_sum_q(0)]
    sum_q.append(start_sum_q(1))
    nys_p += links.start([(piece[1], piece[1], links.along_p(k)) for k in (1, 3)])
    mine = vectors(blocks[0], 256)
    eig_p = links.start([(mine, mine, links.along_p(k)) for k in range(1, 4)])
    arrived(batch_own)
    fill(2304 - c * 256, 1024)
    sum_z = [start_sum_z(0)]
    sum_z.append(start_sum_z(1))
    nys_far = links.start([(nys(blocks[0], 256), nys(blocks[0], 256), links.along_p(2))])
    resid_z = [start_resid_z(0)]
    resid_z.append(start_resid_z(1))
    arrived(nys_p)
    nys_core = links.start(
        [(nys(blocks[k], 256), nys(blocks[k], 256), links.core()) for k in (1, 3)]
    )
    fill(blocks[1], 1280)
    fill(blocks[3], 1280)
    arrived(nys_core)
    fill(theirs[1], 1280)
    resid_q = [start_resid_q(0)]
    resid_q.append(start_resid_q(1))
    arrived(eig_p)
    eig_core = links.start([(vectors(c * 1024, 1024), vectors(c * 1024, 1024), links.core())])
    arrived(nys_far)
    nys_last = links.start([(nys(blocks[2], 256), nys(blocks[2], 256), links.core())])
    fill(theirs[3], 1280)
    fill(blocks[2], 1280, 1024)
    narrow = lax.broadcasted_iota(jnp.int32, (256, 128), 1) < 32

    def split(i, carry):
        rows = at(i * 256, 256)
        some = eig[pl.ds(i * 8, 8), :, :]
        high, middle, low = three(some[:, 0:32, :].reshape(256, 128))
        stack[rows, 0:128] = high
        stack[rows, 128:256] = high
        stack[rows, 256:384] = middle
        stack[rows, 512:640] = low
        rest = some[:, 32:40, :].reshape(64, 128)
        rest = [rest] + [pltpu.roll(rest, 128 - 32 * k, 1) for k in range(1, 4)]
        rest = jnp.concatenate([v.reshape(8, 8, 128) for v in rest], axis=1).reshape(256, 128)
        high, middle, low = three(jnp.where(narrow, rest, 0.0))
        stack[rows, 384:512] = beside(high, high, middle)
        stack[rows, 640:768] = low
        return carry

    lax.fori_loop(c * 4, c * 4 + 4, split, 0)
    resid_p = [start_resid_p(0)]
    resid_p.append(start_resid_p(1))
    arrived(eig_core)
    lax.fori_loop(4 - c * 4, 8 - c * 4, split, 0)
    arrived(nys_last)
    fill(theirs[2], 1280, 1024)

    loads[6].wait()
    wide_corr[...] = jnp.zeros((1, 256), F32)
    wide_corr[:, 0:Q] = small_corr[...]
    product = jnp.dot(table[1024:1280, 0:NYS], stack[...], preferred_element_type=F32)
    value = product[:, 0:128] + product[:, 256:384] + product[:, 512:640]
    high, middle, low = three(value * wide_corr[:, 0:128])
    rows = at(c * 256, 256)
    mixed[rows, 0:128] = high
    mixed[rows, 128:256] = middle
    mixed[rows, 256:384] = low
    value = product[:, 384:512]
    value = value + pltpu.roll(value, 64, 1) + product[:, 640:768]
    high, middle, low = three(jnp.where(narrow, value * wide_corr[:, 128:256], 0.0))
    mixed[rows, 384:512] = beside(high, middle, low)
    mixed_core = links.start([(mixed.at[rows, :], mixed.at[rows, :], links.core())])
    fill(blocks[2], 1024, norms=False)
    fill(theirs[2], 1024, norms=False)
    resid_core = pass_on(0)
    arrived(mixed_core)
    arrived(resid_core)
    project(resid[0:512, :], mixed, scaled)
    resid_core = pass_on(1)
    correct(scaled, stack, coefs)
    arrived(resid_core)
    for copy in links.all:
        copy.wait_send()


def project(resid, mixed, scaled):
    narrow = lax.broadcasted_iota(jnp.int32, (512, 128), 1) < 32
    value = jnp.dot(resid, mixed[...], preferred_element_type=F32)
    high, middle, _ = three(value[:, 0:128] + value[:, 128:256] + value[:, 256:384])
    scaled[:, 0:128] = high
    scaled[:, 128:256] = middle
    scaled[:, 256:384] = high
    value = value[:, 384:512]
    value = value + pltpu.roll(value, 96, 1) + pltpu.roll(value, 64, 1)
    high, middle, _ = three(jnp.where(narrow, value, 0.0))
    scaled[:, 384:512] = beside(high, middle, high)


def correct(scaled, stack, coefs):
    for i in range(4):
        cols = slice(512 * i, 512 * i + 512)
        coefs[:, cols] = (-by_rows(scaled[...], stack[cols, 0:512])).astype(BF16)


def tail_kernel(old, stack, table, mixed, resid, first, out, scaled, coefs, new, sent):
    coefs[0:512, 0:NYS] = first[...]
    project(resid[512:1024, :], mixed, scaled)
    correct(scaled, stack, coefs.at[512:1024, :])
    coefs[:, NYS : NYS + BATCH] = resid[...]
    copies = []
    for i in range(4):
        cols = slice(256 * i, 256 * i + 256)
        for rows in (slice(0, 512), slice(512, OUT)):
            change = by_rows(coefs[rows.start : rows.start + 512, :], table[cols, :])
            new[rows, cols] = old[rows, cols] - (RATE / BATCH) * change[0 : rows.stop - rows.start]
        copies.append(pltpu.make_async_copy(new.at[:, cols], out.at[:, cols], sent.at[i]))
        copies[-1].start()
    for copy in copies:
        copy.wait()


def by_rows(a, b):
    return lax.dot_general(a, b, (((1,), (1,)), ((), ())), preferred_element_type=F32)


def beside(a, b, c):
    a, b, c = (v.astype(F32) for v in (a, b, c))
    return (a + pltpu.roll(b, 32, 1) + pltpu.roll(c, 64, 1)).astype(BF16)


def per_device(centers, weights, batch_points, labels, nystrom_points, eigvecs, corrections):
    hbm = pl.BlockSpec(memory_space=pltpu.HBM)
    vmem = pltpu.VMEM
    inner = pl.BlockSpec(memory_space=vmem)
    handed = pl.pallas_call(
        step_kernel,
        out_shape=(
            jax.ShapeDtypeStruct((NYS, 768), BF16),
            jax.ShapeDtypeStruct((1280, NYS + BATCH), BF16),
            jax.ShapeDtypeStruct((BATCH, 512), BF16),
            jax.ShapeDtypeStruct((1024, BATCH), BF16),
            jax.ShapeDtypeStruct((512, NYS), BF16),
        ),
        in_specs=[hbm] * 7,
        out_specs=(inner,) * 5,
        scratch_shapes=[
            vmem((2304, FEATURES), BF16),
            vmem((1280, 1), F32),
            vmem((2560, FEATURES), BF16),
            vmem((1, 2560), F32),
            vmem((1, 2048), F32),
            vmem((2, FEATURES), BF16),
            vmem((2, OUT), F32),
            vmem((64, Q), F32),
            vmem((1, Q), F32),
            vmem((1, 256), F32),
            vmem((256, FEATURES), BF16),
            vmem((8, 256, 128), F32),
            vmem((8, 256, 128), F32),
            vmem((OUT, CEN), F32),
            vmem((1024, 2048), BF16),
            vmem((64, 40, 128), F32),
            vmem((256, 2048), BF16),
            vmem((1024, 256), F32),
            vmem((1024, 256), F32),
            vmem((2, 128, 256), F32),
            vmem((2, 32, 256), F32),
            vmem((2, 3, 128, 256), F32),
            vmem((2, 3, 32, 256), F32),
            vmem((2, 7, 8, 128), F32),
            vmem((2, 8, 8, 128), F32),
            vmem((512, 512), BF16),
            pltpu.SemaphoreType.DMA((110,)),
            pltpu.SemaphoreType.DMA((110,)),
            pltpu.SemaphoreType.DMA((7,)),
        ],
        compiler_params=pltpu.CompilerParams(
            collective_id=0, has_side_effects=True, vmem_limit_bytes=38 << 20
        ),
        name="step",
    )(
        *(
            pltpu.with_memory_space_constraint(v, pltpu.HBM)
            for v in (
                centers,
                weights.T,
                batch_points,
                labels,
                nystrom_points,
                eigvecs,
                corrections.reshape(1, Q),
            )
        )
    )
    return pl.pallas_call(
        tail_kernel,
        out_shape=jax.ShapeDtypeStruct((OUT, CEN), F32),
        in_specs=[inner] * 6,
        out_specs=hbm,
        scratch_shapes=[
            vmem((512, 512), BF16),
            vmem((1024, NYS + BATCH), BF16),
            vmem((OUT, CEN), F32),
            pltpu.SemaphoreType.DMA((4,)),
        ],
        compiler_params=pltpu.CompilerParams(vmem_limit_bytes=24 << 20),
        name="tail",
    )(weights.T, *handed).T


def solution(mesh):
    every = P(("narrow", "wide", "nys"), None)
    some = P(("narrow", "nys"), None)
    return jax.shard_map(
        per_device,
        mesh=mesh,
        in_specs=(every, every, every, every, some, some, P()),
        out_specs=every,
        check_vma=False,
    )
```

```python
import math

import jax
import jax.numpy as jnp
from jax import lax
from jax.experimental import pallas as pl
from jax.experimental.pallas import tpu as pltpu
from jax.sharding import PartitionSpec as P

RATE = 16.0
SPREAD = 4.0
MESH = pl.DeviceIdType.MESH
F32, BF16 = jnp.float32, jnp.bfloat16

FEATURES = 1024
CEN = 1024
OUT = 1000
NYS = 2048
BATCH = 512
Q = 160
UNIT = (math.log2(math.e) / SPREAD) ** 2
TOP = math.sqrt(2.0 * FEATURES) * math.log2(math.e) / SPREAD


def device(x, y, z, c):
    return (y * 2 + z % 2, (z // 2) * 2 + c, x)


class Links:
    def __init__(self, send, recv):
        n, w, self.x = (lax.axis_index(a) for a in ("narrow", "wide", "nys"))
        self.y, self.c = n // 2, w % 2
        self.z = (w // 2) * 2 + n % 2
        self.p = self.x * (1 - self.c) + self.y * self.c
        self.q = self.y * (1 - self.c) + self.x * self.c
        self.send, self.recv, self.next, self.all = send, recv, 0, []

    def core(self):
        return device(self.x, self.y, self.z, 1 - self.c)

    def along_p(self, k):
        c = self.c
        return device((self.x + k * (1 - c)) % 4, (self.y + k * c) % 4, self.z, c)

    def along_q(self, k):
        c = self.c
        return device((self.x + k * c) % 4, (self.y + k * (1 - c)) % 4, self.z, c)

    def along_z(self, k):
        return device(self.x, self.y, (self.z + k) % 8, self.c)

    def z_pair(self):
        return device(self.x, self.y, self.z + 1 - 2 * (self.z % 2), self.c)

    def peers(self):
        out = [self.core()]
        out += [self.along_p(k) for k in range(1, 4)]
        out += [self.along_q(k) for k in range(1, 4)]
        out += [self.along_z(k) for k in range(1, 8)]
        return out

    def start(self, pairs):
        out = []
        for src, dst, peer in pairs:
            copy = pltpu.make_async_remote_copy(
                src_ref=src,
                dst_ref=dst,
                send_sem=self.send.at[self.next],
                recv_sem=self.recv.at[self.next],
                device_id=peer,
                device_id_type=MESH,
            )
            self.next += 1
            copy.start()
            out.append(copy)
        self.all += out
        return out


def arrived(copies):
    for copy in copies:
        copy.wait_recv()


def at(start, size, unit=None):
    if isinstance(start, int):
        return slice(start, start + size)
    return pl.ds(pl.multiple_of(start, unit or size), size)


def square_sums(points):
    wide = points.astype(F32)
    return jnp.sum(wide * wide, axis=1, keepdims=True) * UNIT


def as_row(column):
    return jnp.transpose(jnp.broadcast_to(column, (column.shape[0], 128)))[0:1, :]


def kernel_values(left, left_sq, right, right_sq):
    cross = lax.dot_general(left, right, (((1,), (1,)), ((), ())), preferred_element_type=F32)
    dist_sq = jnp.maximum((left_sq + right_sq) - (2.0 * UNIT) * cross, 1e-30)
    return jnp.exp2(TOP - dist_sq * lax.rsqrt(dist_sq)).astype(BF16)


def three(value):
    high = value.astype(BF16)
    rest = value - high.astype(F32)
    middle = rest.astype(BF16)
    low = (rest - middle.astype(F32)).astype(BF16)
    return high, middle, low


def step_kernel(
    centers,
    weights,
    batch,
    labels,
    nystrom,
    eigvecs,
    corrections,
    stack,
    table,
    mixed,
    resid,
    coefs,
    left,
    left_sq,
    right,
    right_sq,
    center_sq,
    small_batch,
    small_labels,
    small_eig,
    small_corr,
    wide_corr,
    tiles,
    wide_tiles,
    wide_batch,
    old,
    rounded,
    eig,
    k_batch,
    part,
    placed,
    sum1,
    sum2,
    from_p,
    from_q,
    from_z,
    gathered,
    scaled,
    send,
    recv,
    local,
):
    links = Links(send, recv)
    c, p, q, z = links.c, links.p, links.q, links.z
    group = p * 4 + q

    own_n = c * 1024 + p * 256 + q * 64 + (z % 2) * 32
    loads = [
        (batch, small_batch),
        (labels, small_labels),
        (eigvecs, small_eig),
        (nystrom.at[at(c * 32, 32), :], right.at[at(own_n, 32), :]),
        (centers, left.at[0:1024, :]),
        (weights, old),
        (corrections, small_corr),
    ]
    loads = [pltpu.make_async_copy(s, d, local.at[i]) for i, (s, d) in enumerate(loads)]
    for load in loads:
        load.start()
    barrier = pltpu.get_barrier_semaphore()
    peers = links.peers()
    for peer in peers:
        pl.semaphore_signal(barrier, inc=1, device_id=peer, device_id_type=MESH)

    loads[0].wait()
    pair = small_batch[...].astype(F32)
    for r in range(2):
        for j in range(8):
            wide_tiles[0, 8 * r + j : 8 * r + j + 1, :] = pair[r : r + 1, 128 * j : 128 * j + 128]
    tiles[at(group * 16, 16), at(z * 128, 128)] = wide_tiles[0, 0:16, :].astype(BF16)
    loads[2].wait()
    own_e = own_n // 32
    mine = small_eig[at(c * 32, 32), :]
    eig[own_e, 0:32, :] = mine[:, 0:128]
    for k in range(4):
        eig[own_e, 32:40, 32 * k : 32 * k + 32] = mine[8 * k : 8 * k + 8, 128:Q]
    loads[3].wait()
    pl.semaphore_wait(barrier, len(peers))

    def nys(first, count):
        return right.at[at(first, count, count), :]

    def vectors(first, count):
        return eig.at[pl.ds(first // 32, count // 32)]

    tile = tiles.at[at(group * 16, 16), at(z * 128, 128)]
    batch_q = links.start([(tile, tile, links.along_q(k)) for k in range(1, 4)])
    own = [nys(own_n, 32), vectors(own_n, 32)]
    nys_z = links.start([(o, o, links.z_pair()) for o in own])
    loads[4].wait()
    swap = links.start([(left.at[0:1024, :], left.at[1280:2304, :], links.core())])

    arrived(batch_q)
    tile = tiles.at[at(p * 64, 64), at(z * 128, 128)]
    batch_z = links.start([(tile, tile, links.along_z(k)) for k in range(1, 8)])
    arrived(nys_z)
    own_q = c * 1024 + p * 256 + q * 64
    own = [nys(own_q, 64), vectors(own_q, 64)]
    nys_q = links.start([(o, o, links.along_q(k)) for k in range(1, 4) for o in own])

    loads[5].wait()
    for i in range(7):
        rows = slice(128 * i, 128 * i + 128)
        rounded[rows, 0:1024] = old[rows, :].astype(BF16)
    last = jnp.concatenate([old[896:OUT, :], jnp.zeros((1024 - OUT, CEN), F32)], axis=0)
    rounded[896:1024, 0:1024] = last.astype(BF16)
    swap += links.start([(rounded.at[:, 0:1024], rounded.at[:, 1024:2048], links.core())])

    arrived(batch_z)
    block = tiles.at[at(p * 64, 64), :]
    batch_p = links.start([(block, block, links.along_p(k)) for k in range(1, 4)])

    def own_squares(i, carry):
        rows = at(i * 256, 256)
        value = square_sums(left[rows, :])
        left_sq[rows, :] = value
        center_sq[:, rows] = as_row(value)
        return carry

    lax.fori_loop(0, 4, own_squares, 0)
    loads[1].wait()
    wide_labels = [
        jnp.transpose(jnp.broadcast_to(small_labels[r : r + 1, :], (128, OUT))) for r in range(2)
    ]
    lane = lax.broadcasted_iota(jnp.int32, (OUT, 128), 1)
    for i in range(2):
        point = group * 16 + z - 128 * i
        placed[0:OUT, 128 * i : 128 * i + 128] = jnp.where(
            lane == point, wide_labels[0], jnp.where(lane == point + 8, wide_labels[1], 0.0)
        )
    placed[OUT:1024, :] = jnp.zeros((1024 - OUT, 256), F32)
    arrived(nys_q)
    blocks = [c * 1024 + ((p + k) % 4) * 256 for k in range(4)]
    nys_own = links.start([(nys(blocks[0], 256), nys(blocks[0], 256), links.core())])
    arrived(swap)

    def other_squares(i, carry):
        rows = pl.ds(pl.multiple_of(1280 + i * 256, 256), 256)
        center_sq[:, pl.ds(pl.multiple_of(1024 + i * 256, 256), 256)] = as_row(
            square_sums(left[rows, :])
        )
        return carry

    lax.fori_loop(0, 4, other_squares, 0)
    arrived(batch_p)
    piece = [nys(blocks[0] + 128 * i, 128) for i in range(2)]
    nys_p = links.start([(piece[0], piece[0], links.along_p(k)) for k in (1, 3)])

    for zz in range(8):
        wide_tiles[zz] = tiles[:, 128 * zz : 128 * zz + 128].astype(F32)
    for zz in range(8):
        for j in range(8):
            wide_batch[j, pl.ds(zz, 32, stride=8), :] = wide_tiles[zz, pl.ds(j, 32, stride=8), :]
    squares = jnp.zeros((256, 128), F32)
    for j in range(8):
        wide = wide_batch[j]
        left[1024:1280, 128 * j : 128 * j + 128] = wide.astype(BF16)
        squares = squares + wide * wide
    left_sq[1024:1280, :] = jnp.sum(squares, axis=1, keepdims=True) * UNIT
    points, points_sq = left[1024:1280, :], left_sq[1024:1280, :]
    for i in range(8):
        first = i * 256 if i < 4 else 256 + i * 256
        k_batch[:, 256 * i : 256 * i + 256] = kernel_values(
            points, points_sq, left[first : first + 256, :], center_sq[:, 256 * i : 256 * i + 256]
        )
    scale = (CEN * 256) ** (-0.5)
    sum_p = []
    for h in range(2):
        for i in range(2):
            rows = slice(512 * h + 256 * i, 512 * h + 256 * i + 256)
            part[rows, :] = scale * by_rows(rounded[rows, :], k_batch[...]) - placed[rows, :]
        sum_p.append(
            links.start(
                [
                    (
                        part.at[at(512 * h + ((p + k) % 4) * 128, 128), :],
                        from_p.at[h, k - 1],
                        links.along_p(k),
                    )
                    for k in range(1, 4)
                ]
            )
        )
    own_b = at(2048 + c * 256, 256)
    right[own_b, :] = left[1024:1280, :]
    batch_own = links.start([(right.at[own_b, :], right.at[own_b, :], links.core())])

    def fill(first, end, begin=0, norms=True):
        cols = pl.ds(pl.multiple_of(first, 256), 256)
        if norms:
            right_sq[:, cols] = as_row(square_sums(right[cols, :]))
        count = max((end - begin) // 2, 256)
        for i in range(begin, end, count):
            rows = slice(i, i + count)
            table[rows, cols] = kernel_values(
                left[rows, :], left_sq[rows, :], right[cols, :], right_sq[:, cols]
            )

    theirs = [(1 - c) * 1024 + ((q + k) % 4) * 256 for k in range(4)]
    here = at(c * 256, 256)

    def start_sum_q(h):
        arrived(sum_p[h])
        for i in range(2):
            rows = slice(64 * i, 64 * i + 64)
            sum1[h, rows, :] = (
                part[at(512 * h + p * 128 + 64 * i, 64), :]
                + from_p[h, 0, rows, :]
                + from_p[h, 1, rows, :]
                + from_p[h, 2, rows, :]
            )
        return links.start(
            [
                (
                    sum1.at[h, at(((q + k) % 4) * 32, 32), :],
                    from_q.at[h, k - 1],
                    links.along_q(k),
                )
                for k in range(1, 4)
            ]
        )

    def share(h, owner):
        return sum2.at[h, at((owner // 2) * 8, 8), at((owner % 2) * 128, 128)]

    def start_sum_z(h):
        arrived(sum_q[h])
        sum2[h] = sum1[h, at(q * 32, 32), :] + from_q[h, 0] + from_q[h, 1] + from_q[h, 2]
        return links.start(
            [
                (share(h, (z + k) % 8), from_z.at[h, k - 1], links.along_z(k))
                for k in range(1, 8)
            ]
        )

    def start_resid_z():
        totals = []
        for h in range(2):
            arrived(sum_z[h])
            total = share(h, z)[...]
            for k in range(7):
                total = total + from_z[h, k]
            totals.append(total)
        gathered[z] = jnp.concatenate(totals, axis=0).astype(BF16)
        tile = gathered.at[z]
        return links.start([(tile, tile, links.along_z(k)) for k in range(1, 8)])

    def resid_rows(h, first, count):
        return resid.at[at(512 * h + first, count), here]

    def start_resid_q(h):
        rows = []
        for i in range(0, 8, 2):
            pair = [gathered[i + m].astype(F32)[8 * h : 8 * h + 8] for m in range(2)]
            rows.append(jnp.concatenate(pair, axis=1))
        tile = resid_rows(h, p * 128 + q * 32, 32)
        tile[...] = jnp.concatenate(rows, axis=0).astype(BF16)
        return links.start([(tile, tile, links.along_q(k)) for k in range(1, 4)])

    def start_resid_p(h):
        arrived(resid_q[h])
        tile = resid_rows(h, p * 128, 128)
        out = links.start([(tile, tile, links.along_p(k)) for k in range(1, 4)])
        return out, links.start([(tile, tile, links.core())])

    def pass_on(h):
        copies, more = resid_p[h]
        for k, copy in zip((1, 2, 3), copies):
            arrived([copy])
            tile = resid_rows(h, ((p + 4 - k) % 4) * 128, 128)
            more += links.start([(tile, tile, links.core())])
        return more

    fill(blocks[0], 1280)
    arrived(nys_own)
    fill(theirs[0], 1280)
    fill(2048 + c * 256, 1024)
    sum_q = [start_sum_q(0)]
    sum_q.append(start_sum_q(1))
    nys_p += links.start([(piece[1], piece[1], links.along_p(k)) for k in (1, 3)])
    mine = vectors(blocks[0], 256)
    eig_p = links.start([(mine, mine, links.along_p(k)) for k in range(1, 4)])
    arrived(batch_own)
    fill(2304 - c * 256, 1024)
    sum_z = [start_sum_z(0)]
    sum_z.append(start_sum_z(1))
    nys_far = links.start([(nys(blocks[0], 256), nys(blocks[0], 256), links.along_p(2))])
    resid_z = start_resid_z()
    arrived(nys_p)
    nys_core = links.start(
        [(nys(blocks[k], 256), nys(blocks[k], 256), links.core()) for k in (1, 3)]
    )
    fill(blocks[1], 1280)
    fill(blocks[3], 1280)
    arrived(nys_core)
    fill(theirs[1], 1280)
    arrived(resid_z)
    resid_q = [start_resid_q(0)]
    resid_q.append(start_resid_q(1))
    arrived(eig_p)
    eig_core = links.start([(vectors(c * 1024, 1024), vectors(c * 1024, 1024), links.core())])
    arrived(nys_far)
    nys_last = links.start([(nys(blocks[2], 256), nys(blocks[2], 256), links.core())])
    fill(theirs[3], 1280)
    fill(blocks[2], 1280, 1024)
    narrow = lax.broadcasted_iota(jnp.int32, (256, 128), 1) < 32

    def split(i, carry):
        rows = at(i * 256, 256)
        some = eig[pl.ds(i * 8, 8), :, :]
        high, middle, low = three(some[:, 0:32, :].reshape(256, 128))
        stack[rows, 0:128] = high
        stack[rows, 128:256] = high
        stack[rows, 256:384] = middle
        stack[rows, 512:640] = low
        rest = some[:, 32:40, :].reshape(64, 128)
        rest = [rest] + [pltpu.roll(rest, 128 - 32 * k, 1) for k in range(1, 4)]
        rest = jnp.concatenate([v.reshape(8, 8, 128) for v in rest], axis=1).reshape(256, 128)
        high, middle, low = three(jnp.where(narrow, rest, 0.0))
        stack[rows, 384:512] = beside(high, high, middle)
        stack[rows, 640:768] = low
        return carry

    lax.fori_loop(c * 4, c * 4 + 4, split, 0)
    resid_p = [start_resid_p(0)]
    resid_p.append(start_resid_p(1))
    arrived(eig_core)
    lax.fori_loop(4 - c * 4, 8 - c * 4, split, 0)
    arrived(nys_last)
    fill(theirs[2], 1280, 1024)

    loads[6].wait()
    wide_corr[...] = jnp.zeros((1, 256), F32)
    wide_corr[:, 0:Q] = small_corr[...]
    product = jnp.dot(table[1024:1280, 0:NYS], stack[...], preferred_element_type=F32)
    value = product[:, 0:128] + product[:, 256:384] + product[:, 512:640]
    high, middle, low = three(value * wide_corr[:, 0:128])
    rows = at(c * 256, 256)
    mixed[rows, 0:128] = high
    mixed[rows, 128:256] = middle
    mixed[rows, 256:384] = low
    value = product[:, 384:512]
    value = value + pltpu.roll(value, 64, 1) + product[:, 640:768]
    high, middle, low = three(jnp.where(narrow, value * wide_corr[:, 128:256], 0.0))
    mixed[rows, 384:512] = beside(high, middle, low)
    mixed_core = links.start([(mixed.at[rows, :], mixed.at[rows, :], links.core())])
    fill(blocks[2], 1024, norms=False)
    fill(theirs[2], 1024, norms=False)
    resid_core = pass_on(0)
    arrived(mixed_core)
    arrived(resid_core)
    project(resid[0:512, :], mixed, scaled)
    resid_core = pass_on(1)
    correct(scaled, stack, coefs)
    arrived(resid_core)
    for copy in links.all:
        copy.wait_send()


def project(resid, mixed, scaled):
    narrow = lax.broadcasted_iota(jnp.int32, (512, 128), 1) < 32
    value = jnp.dot(resid, mixed[...], preferred_element_type=F32)
    high, middle, _ = three(value[:, 0:128] + value[:, 128:256] + value[:, 256:384])
    scaled[:, 0:128] = high
    scaled[:, 128:256] = middle
    scaled[:, 256:384] = high
    value = value[:, 384:512]
    value = value + pltpu.roll(value, 96, 1) + pltpu.roll(value, 64, 1)
    high, middle, _ = three(jnp.where(narrow, value, 0.0))
    scaled[:, 384:512] = beside(high, middle, high)


def correct(scaled, stack, coefs):
    for i in range(4):
        cols = slice(512 * i, 512 * i + 512)
        coefs[:, cols] = (-by_rows(scaled[...], stack[cols, 0:512])).astype(BF16)


def tail_kernel(old, stack, table, mixed, resid, first, out, scaled, coefs, new, sent):
    coefs[0:512, 0:NYS] = first[...]
    project(resid[512:1024, :], mixed, scaled)
    correct(scaled, stack, coefs.at[512:1024, :])
    coefs[:, NYS : NYS + BATCH] = resid[...]
    copies = []
    for i in range(4):
        cols = slice(256 * i, 256 * i + 256)
        for rows in (slice(0, 512), slice(512, OUT)):
            change = by_rows(coefs[rows.start : rows.start + 512, :], table[cols, :])
            new[rows, cols] = old[rows, cols] - (RATE / BATCH) * change[0 : rows.stop - rows.start]
        copies.append(pltpu.make_async_copy(new.at[:, cols], out.at[:, cols], sent.at[i]))
        copies[-1].start()
    for copy in copies:
        copy.wait()


def by_rows(a, b):
    return lax.dot_general(a, b, (((1,), (1,)), ((), ())), preferred_element_type=F32)


def beside(a, b, c):
    a, b, c = (v.astype(F32) for v in (a, b, c))
    return (a + pltpu.roll(b, 32, 1) + pltpu.roll(c, 64, 1)).astype(BF16)


def per_device(centers, weights, batch_points, labels, nystrom_points, eigvecs, corrections):
    hbm = pl.BlockSpec(memory_space=pltpu.HBM)
    vmem = pltpu.VMEM
    inner = pl.BlockSpec(memory_space=vmem)
    handed = pl.pallas_call(
        step_kernel,
        out_shape=(
            jax.ShapeDtypeStruct((NYS, 768), BF16),
            jax.ShapeDtypeStruct((1280, NYS + BATCH), BF16),
            jax.ShapeDtypeStruct((BATCH, 512), BF16),
            jax.ShapeDtypeStruct((1024, BATCH), BF16),
            jax.ShapeDtypeStruct((512, NYS), BF16),
        ),
        in_specs=[hbm] * 7,
        out_specs=(inner,) * 5,
        scratch_shapes=[
            vmem((2304, FEATURES), BF16),
            vmem((1280, 1), F32),
            vmem((2560, FEATURES), BF16),
            vmem((1, 2560), F32),
            vmem((1, 2048), F32),
            vmem((2, FEATURES), BF16),
            vmem((2, OUT), F32),
            vmem((64, Q), F32),
            vmem((1, Q), F32),
            vmem((1, 256), F32),
            vmem((256, FEATURES), BF16),
            vmem((8, 256, 128), F32),
            vmem((8, 256, 128), F32),
            vmem((OUT, CEN), F32),
            vmem((1024, 2048), BF16),
            vmem((64, 40, 128), F32),
            vmem((256, 2048), BF16),
            vmem((1024, 256), F32),
            vmem((1024, 256), F32),
            vmem((2, 128, 256), F32),
            vmem((2, 32, 256), F32),
            vmem((2, 3, 128, 256), F32),
            vmem((2, 3, 32, 256), F32),
            vmem((2, 7, 8, 128), F32),
            vmem((8, 16, 128), BF16),
            vmem((512, 512), BF16),
            pltpu.SemaphoreType.DMA((110,)),
            pltpu.SemaphoreType.DMA((110,)),
            pltpu.SemaphoreType.DMA((7,)),
        ],
        compiler_params=pltpu.CompilerParams(
            collective_id=0, has_side_effects=True, vmem_limit_bytes=38 << 20
        ),
        name="step",
    )(
        *(
            pltpu.with_memory_space_constraint(v, pltpu.HBM)
            for v in (
                centers,
                weights.T,
                batch_points,
                labels,
                nystrom_points,
                eigvecs,
                corrections.reshape(1, Q),
            )
        )
    )
    return pl.pallas_call(
        tail_kernel,
        out_shape=jax.ShapeDtypeStruct((OUT, CEN), F32),
        in_specs=[inner] * 6,
        out_specs=hbm,
        scratch_shapes=[
            vmem((512, 512), BF16),
            vmem((1024, NYS + BATCH), BF16),
            vmem((OUT, CEN), F32),
            pltpu.SemaphoreType.DMA((4,)),
        ],
        compiler_params=pltpu.CompilerParams(vmem_limit_bytes=24 << 20),
        name="tail",
    )(weights.T, *handed).T


def solution(mesh):
    every = P(("narrow", "wide", "nys"), None)
    some = P(("narrow", "nys"), None)
    return jax.shard_map(
        per_device,
        mesh=mesh,
        in_specs=(every, every, every, every, some, some, P()),
        out_specs=every,
        check_vma=False,
    )
```
